768 devices in a mesh: gx: 96 (over y, z), gy: 8 (over x, core).
Axes of the slice: x: 4, y: 8, z: 12, core: 2. Of those that a mesh axis runs over, the one named last changes fastest.
Arguments:
- concentration: float32 [16, 768, 1024], P(None, 'gx', 'gy'), may hold values from 0 to 1
- labels: int32 [16, 768, 1024], P(None, 'gx', 'gy'), may hold values from 1 to 4096
- curve_scale: float32 [8], replicated, may hold values from 0.3 to 3
- curve_slope: float32 [8], replicated, may hold values from -1.5 to 1.5
- coarse_inv: float32 [8, 6144, 6144], P('gy', 'gx'), may hold values from -1 to 1.3, as said below
Outputs:
- updated: float32 [16, 768, 1024], P(None, 'gx', 'gy')
- residual: float32 [16, 768, 1024], P(None, 'gx', 'gy')
The draws below stay inside these ranges and needn't reach their ends.
Inputs may be any that keep to these rules, and one draw needn't show every extreme that they name: `coarse_inv`: symmetric and positive definite for each column of subdomains.
All inputs are finite; a program needn't handle non-finite values.
Results may differ from the reference program's by a relative error of at most 0.0003.
Values sent between devices are 32-bit elements; how exact they have to be, the bound alone decides.
No kernel may reach another device: no remote copies, remote signals or barrier semaphores. Data moves between devices by JAX's collectives and lax.ppermute only.
A program may use at most 32 MiB of HBM per device.

```python
import math
import jax
import jax.numpy as jnp
from jax import lax

NZ = 16
CX = 8
CY = 128
OV = 2
SWEEPS = 3
CHEB = 4
MZ = 2
MX = 4
MY = 8
KINDS = 8
PARTICLES = 4096
NB = 64
NX = 768
NY = 1024
NC = 6144
COLS = 8
N_GX = 96
N_GY = 8


def draw_concentration(key, part):
    roughness = jax.random.uniform(jax.random.fold_in(key, 11), (NZ, NX, NY), jnp.float32)
    return roughness


def draw_labels(key, part):
    shift_first = jax.random.randint(jax.random.fold_in(key, 21), (), 0, 24)
    shift_second = jax.random.randint(jax.random.fold_in(key, 22), (), 0, 40)
    boxes_first = NX // 24 + 2
    boxes_second = NY // 40 + 2
    boxes_depth = NZ // 8 + 1
    box_labels = jax.random.randint(jax.random.fold_in(key, 23), (boxes_depth, boxes_first, boxes_second), 1, PARTICLES + 1)
    box_labels = box_labels.at[0, 0, 0].set(PARTICLES)
    box_labels = box_labels.at[1, 0, 0].set(1)
    box_first = (jnp.arange(NX, dtype=jnp.int32) + shift_first) // 24
    box_second = (jnp.arange(NY, dtype=jnp.int32) + shift_second) // 40
    box_depth = jnp.arange(NZ, dtype=jnp.int32) // 8
    return box_labels[box_depth[:, None, None], box_first[None, :, None], box_second[None, None, :]]


def draw_coarse_inv(key, part):
    raw_values = jax.random.normal(jax.random.fold_in(key, 31), (COLS, NC, NC), jnp.float32)
    diagonal = jax.random.uniform(jax.random.fold_in(key, 32), (COLS, NC), jnp.float32, 0.8, 1.2)
    symmetric = (raw_values + jnp.swapaxes(raw_values, 1, 2)) * (0.2 / math.sqrt(NC))
    identity = jnp.eye(NC, dtype=jnp.float32)
    return symmetric * (1.0 - identity)[None] + diagonal[:, :, None] * identity[None]


def setup_inputs(seed: int = 0) -> dict:
    keys = jax.random.split(jax.random.key(seed), 6)
    return {
        "concentration": draw_concentration(jax.random.fold_in(keys[5], 71), 0),
        "labels": draw_labels(jax.random.fold_in(keys[5], 71), 0),
        "curve_scale": jnp.clip(jnp.exp(jax.random.uniform(keys[2], (KINDS,), jnp.float32, math.log(0.3), math.log(3.0))), 0.3, 3.0),
        "curve_slope": jnp.clip(jax.random.uniform(keys[3], (KINDS,), jnp.float32, -1.5, 1.5), -1.5, 1.5),
        "coarse_inv": draw_coarse_inv(jax.random.fold_in(keys[5], 71), 0),
    }


INVERSE_STEP = 0.004
CONTACT = 0.3
LOWER_BOUND = 0.1
UPPER_BOUND = 1.9

def pad_frame(values, margin):
    return jnp.pad(values, ((0, 0), (margin, margin), (margin, margin)))

def pair_weight(first_coeff, second_coeff, first_label, second_label):
    inside = jnp.where(first_label > 0.5, 1.0, 0.0) * jnp.where(second_label > 0.5, 1.0, 0.0)
    return 0.5 * (first_coeff + second_coeff) * inside * jnp.where(first_label == second_label, 1.0, CONTACT)

def face_weights(coeff_box, label_box):
    mid_coeff = coeff_box[:, 1:-1, 1:-1]
    mid_label = label_box[:, 1:-1, 1:-1]
    west_weight = pair_weight(mid_coeff, coeff_box[:, :-2, 1:-1], mid_label, label_box[:, :-2, 1:-1])
    east_weight = pair_weight(mid_coeff, coeff_box[:, 2:, 1:-1], mid_label, label_box[:, 2:, 1:-1])
    south_weight = pair_weight(mid_coeff, coeff_box[:, 1:-1, :-2], mid_label, label_box[:, 1:-1, :-2])
    north_weight = pair_weight(mid_coeff, coeff_box[:, 1:-1, 2:], mid_label, label_box[:, 1:-1, 2:])
    vertical = pair_weight(mid_coeff[:-1], mid_coeff[1:], mid_label[:-1], mid_label[1:])
    zero_layer = jnp.zeros_like(mid_coeff[:1])
    below_weight = jnp.concatenate([zero_layer, vertical], 0)
    above_weight = jnp.concatenate([vertical, zero_layer], 0)
    weights = (west_weight, east_weight, south_weight, north_weight, below_weight, above_weight)
    diagonal = INVERSE_STEP + west_weight + east_weight + south_weight + north_weight + below_weight + above_weight
    return (weights, diagonal)

def apply_op(field_box, weights, diagonal):
    west_weight, east_weight, south_weight, north_weight, below_weight, above_weight = weights
    centre_cells = field_box[:, 1:-1, 1:-1]
    zero_layer = jnp.zeros_like(centre_cells[:1])
    below_cells = jnp.concatenate([zero_layer, centre_cells[:-1]], 0)
    above_cells = jnp.concatenate([centre_cells[1:], zero_layer], 0)
    beside = west_weight * field_box[:, :-2, 1:-1] + east_weight * field_box[:, 2:, 1:-1]
    beside = beside + south_weight * field_box[:, 1:-1, :-2] + north_weight * field_box[:, 1:-1, 2:]
    beside = beside + below_weight * below_cells + above_weight * above_cells
    return diagonal * centre_cells - beside

def smooth_local(residual_box, weights, diagonal):
    centre = (UPPER_BOUND + LOWER_BOUND) / 2.0
    radius = (UPPER_BOUND - LOWER_BOUND) / 2.0
    spread = centre / radius
    ratio_now = 1.0 / spread
    inverse = 1.0 / diagonal
    update = inverse * residual_box / centre
    result = update
    remain = residual_box
    for iteration in range(CHEB - 1):
        remain = remain - apply_op(pad_frame(update, 1), weights, diagonal)
        ratio_next = 1.0 / (2.0 * spread - ratio_now)
        update = ratio_next * ratio_now * update + 2.0 * ratio_next / radius * inverse * remain
        result = result + update
        ratio_now = ratio_next
    return result

def cosine_table(mode_count, length):
    position = jnp.arange(length, dtype=jnp.float32) + 0.5
    order = jnp.arange(mode_count, dtype=jnp.float32)
    scaling = jnp.where(order == 0, math.sqrt(1.0 / length), math.sqrt(2.0 / length))
    return scaling[:, None] * jnp.cos(math.pi * order[:, None] * position[None, :] / length)

def local_sweeps(residual_pad, weights, diagonal):

    def solve_block(block_index):
        row_index = (block_index // N_GY).astype(jnp.int32)
        col_index = (block_index % N_GY).astype(jnp.int32)
        anchor = jnp.zeros((), jnp.int32)

        def cut_box(values):
            return lax.dynamic_slice(values, (anchor, row_index * CX, col_index * CY), (NZ, CX + 2 * OV, CY + 2 * OV))
        result = smooth_local(cut_box(residual_pad), tuple((cut_box(w) for w in weights)), cut_box(diagonal))
        return result[:, OV:OV + CX, OV:OV + CY]
    blocks = lax.map(solve_block, jnp.arange(N_GX * N_GY, dtype=jnp.int32))
    return blocks.reshape(N_GX, N_GY, NZ, CX, CY).transpose(2, 0, 3, 1, 4).reshape(NZ, NX, NY)

def coarse_part(residual_own, coarse_inv):
    depth_table = cosine_table(MZ, NZ)
    first_table = cosine_table(MX, CX)
    second_table = cosine_table(MY, CY)
    blocks = residual_own.reshape(NZ, N_GX, CX, N_GY, CY)
    moments = jnp.einsum('sz,px,qy,zaxby->baspq', depth_table, first_table, second_table, blocks, precision=lax.Precision.HIGHEST).reshape(N_GY, N_GX * NB)
    answer = jnp.einsum('bij,bj->bi', coarse_inv, moments, precision=lax.Precision.HIGHEST)
    answer = answer.reshape(N_GY, N_GX, MZ, MX, MY)
    field = jnp.einsum('sz,px,qy,baspq->zaxby', depth_table, first_table, second_table, answer, precision=lax.Precision.HIGHEST)
    return field.reshape(NZ, NX, NY)

def interior(values):
    return values[:, OV:-OV, OV:-OV]

def reference(concentration, labels, curve_scale, curve_slope, coarse_inv):
    material = labels % KINDS
    diffusivity = curve_scale[material] * jnp.exp(curve_slope[material] * concentration)
    label_values = labels.astype(jnp.float32)
    frame_width = OV + 1
    weights, diagonal = face_weights(pad_frame(diffusivity, frame_width), pad_frame(label_values, frame_width))
    conc_frame = pad_frame(concentration, frame_width)
    source = INVERSE_STEP * conc_frame[:, 1:-1, 1:-1] - apply_op(conc_frame, weights, diagonal)
    own_weights = tuple((interior(w) for w in weights))
    own_diagonal = interior(diagonal)
    source_own = interior(source)
    newton_update = jnp.zeros_like(concentration)
    residual_pad = source
    for sweep_index in range(SWEEPS):
        if sweep_index > 0:
            residual_own = source_own - apply_op(pad_frame(newton_update, 1), own_weights, own_diagonal)
            residual_pad = pad_frame(residual_own, OV)
        residual_own = interior(residual_pad)
        local_part = local_sweeps(residual_pad, weights, diagonal)
        newton_update = newton_update + local_part + coarse_part(residual_own, coarse_inv)
    residual_last = source_own - apply_op(pad_frame(newton_update, 1), own_weights, own_diagonal)
    return (concentration + newton_update, residual_last)
```

```python
import math

import jax
import jax.numpy as jnp
from jax import lax
from jax.sharding import PartitionSpec as P

OV = 2
SWEEPS = 3
CHEB = 4
MZ = 2
MX = 4
MY = 8
KINDS = 8
N_Y = 8
N_Z = 12


INVERSE_STEP = 0.004
CONTACT = 0.3
LOWER_BOUND = 0.1
UPPER_BOUND = 1.9


def extended(array, sides, width):
    for axis, dim in sides:
        size, length = (lax.axis_size(axis), array.shape[dim])
        up = [(i, (i + 1) % size) for i in range(size - 1)]
        down = [(j, i) for i, j in up]
        last = lax.slice_in_dim(array, length - width, length, axis=dim)
        initial = lax.slice_in_dim(array, 0, width, axis=dim)
        before = lax.ppermute(last, axis, up)
        after = lax.ppermute(initial, axis, down)
        array = jnp.concatenate([before, array, after], axis=dim)
    return array


def pad_frame(values, margin):
    return jnp.pad(values, ((0, 0), (margin, margin), (margin, margin)))


def pair_weight(first_coeff, second_coeff, first_label, second_label):
    inside = jnp.where(first_label > 0.5, 1.0, 0.0) * jnp.where(second_label > 0.5, 1.0, 0.0)
    return (
        0.5
        * (first_coeff + second_coeff)
        * inside
        * jnp.where(first_label == second_label, 1.0, CONTACT)
    )


def face_weights(coeff_box, label_box):
    mid_coeff = coeff_box[:, 1:-1, 1:-1]
    mid_label = label_box[:, 1:-1, 1:-1]
    west_weight = pair_weight(
        mid_coeff, coeff_box[:, :-2, 1:-1], mid_label, label_box[:, :-2, 1:-1]
    )
    east_weight = pair_weight(mid_coeff, coeff_box[:, 2:, 1:-1], mid_label, label_box[:, 2:, 1:-1])
    south_weight = pair_weight(
        mid_coeff, coeff_box[:, 1:-1, :-2], mid_label, label_box[:, 1:-1, :-2]
    )
    north_weight = pair_weight(mid_coeff, coeff_box[:, 1:-1, 2:], mid_label, label_box[:, 1:-1, 2:])
    vertical = pair_weight(mid_coeff[:-1], mid_coeff[1:], mid_label[:-1], mid_label[1:])
    zero_layer = jnp.zeros_like(mid_coeff[:1])
    below_weight = jnp.concatenate([zero_layer, vertical], 0)
    above_weight = jnp.concatenate([vertical, zero_layer], 0)
    weights = (west_weight, east_weight, south_weight, north_weight, below_weight, above_weight)
    diagonal = (
        INVERSE_STEP
        + west_weight
        + east_weight
        + south_weight
        + north_weight
        + below_weight
        + above_weight
    )
    return (weights, diagonal)


def apply_op(field_box, weights, diagonal):
    west_weight, east_weight, south_weight, north_weight, below_weight, above_weight = weights
    centre_cells = field_box[:, 1:-1, 1:-1]
    zero_layer = jnp.zeros_like(centre_cells[:1])
    below_cells = jnp.concatenate([zero_layer, centre_cells[:-1]], 0)
    above_cells = jnp.concatenate([centre_cells[1:], zero_layer], 0)
    beside = west_weight * field_box[:, :-2, 1:-1] + east_weight * field_box[:, 2:, 1:-1]
    beside = beside + south_weight * field_box[:, 1:-1, :-2] + north_weight * field_box[:, 1:-1, 2:]
    beside = beside + below_weight * below_cells + above_weight * above_cells
    return diagonal * centre_cells - beside


def smooth_local(residual_box, weights, diagonal):
    centre = (UPPER_BOUND + LOWER_BOUND) / 2.0
    radius = (UPPER_BOUND - LOWER_BOUND) / 2.0
    spread = centre / radius
    ratio_now = 1.0 / spread
    inverse = 1.0 / diagonal
    update = inverse * residual_box / centre
    result = update
    remain = residual_box
    for iteration in range(CHEB - 1):
        remain = remain - apply_op(pad_frame(update, 1), weights, diagonal)
        ratio_next = 1.0 / (2.0 * spread - ratio_now)
        update = ratio_next * ratio_now * update + 2.0 * ratio_next / radius * inverse * remain
        result = result + update
        ratio_now = ratio_next
    return result


def cosine_table(mode_count, length):
    position = jnp.arange(length, dtype=jnp.float32) + 0.5
    order = jnp.arange(mode_count, dtype=jnp.float32)
    scaling = jnp.where(order == 0, math.sqrt(1.0 / length), math.sqrt(2.0 / length))
    return scaling[:, None] * jnp.cos(math.pi * order[:, None] * position[None, :] / length)


def interior(values):
    return values[:, OV:-OV, OV:-OV]


def gathered(moments):
    along_z = [[y * N_Z + z for z in range(N_Z)] for y in range(N_Y)]
    along_y = [[y * N_Z + z for y in range(N_Y)] for z in range(N_Z)]
    size = moments.shape[0]
    line = lax.all_to_all(
        jnp.broadcast_to(moments[None], (N_Z, size)), "gx", 0, 0, tiled=True, axis_index_groups=along_z
    )
    return lax.all_to_all(
        jnp.broadcast_to(line.reshape(1, N_Z * size), (N_Y, N_Z * size)),
        "gx",
        0,
        0,
        tiled=True,
        axis_index_groups=along_y,
    ).reshape(-1)


def coarse_part(residual_own, own_rows):
    depth_table = cosine_table(MZ, residual_own.shape[0])
    first_table = cosine_table(MX, residual_own.shape[1])
    second_table = cosine_table(MY, residual_own.shape[2])
    moments = jnp.einsum(
        "sz,px,qy,zxy->spq",
        depth_table,
        first_table,
        second_table,
        residual_own,
        precision=lax.Precision.HIGHEST,
    ).reshape(-1)
    answer = jnp.sum(own_rows * gathered(moments)[None], axis=1)
    return jnp.einsum(
        "sz,px,qy,spq->zxy",
        depth_table,
        first_table,
        second_table,
        answer.reshape(MZ, MX, MY),
        precision=lax.Precision.HIGHEST,
    )


def on_device(concentration, labels, curve_scale, curve_slope, coarse_inv):
    frame_width = OV + 1
    material = labels % KINDS
    selector = material[None] == jnp.arange(KINDS, dtype=jnp.int32)[:, None, None, None]
    scale_cells = jnp.sum(jnp.where(selector, curve_scale[:, None, None, None], 0.0), 0)
    slope_cells = jnp.sum(jnp.where(selector, curve_slope[:, None, None, None], 0.0), 0)
    diffusivity = scale_cells * jnp.exp(slope_cells * concentration)
    stacked = jnp.stack([concentration, diffusivity, labels.astype(jnp.float32)])
    framed = extended(stacked, (("gx", 2), ("gy", 3)), frame_width)
    weights, diagonal = face_weights(framed[1], framed[2])
    source = INVERSE_STEP * framed[0][:, 1:-1, 1:-1] - apply_op(framed[0], weights, diagonal)
    own_weights = tuple((interior(w) for w in weights))
    own_diagonal = interior(diagonal)
    source_own = interior(source)
    own_rows = coarse_inv[0]

    def own_residual(newton_update):
        rim_update = extended(newton_update, (("gx", 1), ("gy", 2)), 1)
        return source_own - apply_op(rim_update, own_weights, own_diagonal)

    def box_residual(newton_update):
        frame_update = extended(newton_update, (("gx", 1), ("gy", 2)), frame_width)
        return source - apply_op(frame_update, weights, diagonal)

    newton_update = jnp.zeros_like(concentration)
    residual_box = source
    for sweep_index in range(SWEEPS):
        if sweep_index > 0:
            residual_box = box_residual(newton_update)
        residual_own = interior(residual_box)
        local_part = interior(smooth_local(residual_box, weights, diagonal))
        newton_update = newton_update + local_part + coarse_part(residual_own, own_rows)
    residual_last = own_residual(newton_update)
    return (concentration + newton_update, residual_last)


def solution(mesh):
    return jax.shard_map(
        on_device,
        mesh=mesh,
        in_specs=(P(None, "gx", "gy"), P(None, "gx", "gy"), P(), P(), P("gy", "gx", None)),
        out_specs=(P(None, "gx", "gy"), P(None, "gx", "gy")),
        check_vma=False,
    )
```

```python
import functools
import math

import jax
import jax.numpy as jnp
import numpy as np
from jax import lax
from jax.experimental import pallas as pl
from jax.experimental.pallas import tpu as pltpu
from jax.sharding import PartitionSpec as P

NZ = 16
CX = 8
CY = 128
OV = 2
SWEEPS = 3
CHEB = 4
MZ = 2
MX = 4
MY = 8
NB = 64
N_Z = 12
INVERSE_STEP = 0.004
CONTACT = 0.3
LOWER_BOUND = 0.1
UPPER_BOUND = 1.9

HALO = 13
ROWS = CX + 2 * HALO
FAR = HALO - CX
LANES = 256
STRIP = 16
WINDOW = 8
SPAN = 3
REACH = (8, 4, 0)
PACKS = 9


def cosine_table(mode_count, length):
    position = np.arange(length) + 0.5
    order = np.arange(mode_count)
    scaling = np.where(order == 0, math.sqrt(1.0 / length), math.sqrt(2.0 / length))
    return scaling[:, None] * np.cos(math.pi * order[:, None] * position[None, :] / length)


def tables():
    depth, first, second = cosine_table(MZ, NZ), cosine_table(MX, CX), cosine_table(MY, CY)
    flat = depth[0, 0]
    mix = np.zeros((NB, MZ * CX))
    rows = np.zeros((NB, CY))
    for s in range(MZ):
        for p in range(MX):
            for q in range(MY):
                n = (s * MX + p) * MY + q
                mix[n, s * CX : (s + 1) * CX] = first[p] * (flat if s == 0 else 1.0)
                rows[n] = second[q]
    half = np.zeros((2, CX, 2 * NB))
    spread = np.zeros((2 * NB, MZ, CY))
    for h in range(2):
        for s in range(MZ):
            for p in range(MX):
                for q in range(MY):
                    n = h * NB + (s * MX + p) * MY + q
                    half[h, :, n] = first[p]
                    spread[n, s] = second[q] * (flat if s == 0 else 1.0)
    own = np.zeros((2 * NB, MZ, LANES))
    own[:, :, :CY] = spread
    own[:, :, CY + 13 : CY + 16] = spread[:, :, 125:128]
    own[:, :, CY + 112 : CY + 115] = spread[:, :, 0:3]
    side = np.zeros((2, 2 * NB, MZ, CY))
    side[0, :, :, 96:112] = spread[:, :, 112:128]
    side[0, :, :, 125:128] = spread[:, :, 125:128]
    side[1, :, :, 16:32] = spread[:, :, 0:16]
    side[1, :, :, 0:3] = spread[:, :, 0:3]
    wave = np.broadcast_to(depth[1][:, None], (NZ, CY))
    mix = np.pad(mix, ((0, 0), (0, CY - MZ * CX)))
    parts = [own[:, s, k * CY : (k + 1) * CY] for s in range(MZ) for k in range(2)]
    parts += [side[:, :, s].reshape(4 * NB, CY) for s in range(MZ)]
    parts += [rows, mix, half.reshape(2 * CX, 2 * NB), wave]
    return np.concatenate(parts, axis=0).astype(np.float32)


OWN, SIDE, MOMENT, MIX, HALF, WAVE = 0, 512, 1024, 1088, 1152, 1168


def lane_shift(values, by):
    return pltpu.roll(values, by % values.shape[-1], axis=values.ndim - 1)


def depth_shift(values, by):
    return pltpu.roll(values, by % NZ, axis=0)


def lanes_in(shape, *ranges):
    lane = lax.broadcasted_iota(jnp.int32, shape, len(shape) - 1)
    inside = jnp.zeros(shape, jnp.bool_)
    for low, high in ranges:
        inside = inside | ((lane >= low) & (lane < high))
    return inside


def chebyshev():
    centre = (UPPER_BOUND + LOWER_BOUND) / 2.0
    radius = (UPPER_BOUND - LOWER_BOUND) / 2.0
    spread = centre / radius
    ratio = 1.0 / spread
    steps = []
    for _ in range(CHEB - 1):
        following = 1.0 / (2.0 * spread - ratio)
        steps.append((following * ratio, 2.0 * following / radius))
        ratio = following
    return 1.0 / centre, steps


def side_flux(values, south, below):
    across = south * (values - lane_shift(values, 1))
    upward = below * (values - depth_shift(values, 1))
    return (across - lane_shift(across, -1)) + (upward - depth_shift(upward, -1))


def spread_moments(r_row, table_ref, inv_ref, line_ref, out_ref):
    for x in range(CX):
        row = r_row(x)
        line_ref[x : x + 1, :] = jnp.sum(row, axis=0, keepdims=True)
        line_ref[CX + x : CX + x + 1, :] = jnp.sum(row * table_ref[WAVE : WAVE + NZ, :], axis=0, keepdims=True)
    mix = table_ref[MIX : MIX + NB, : MZ * CX]
    mixed = jnp.dot(mix, line_ref[...], precision=lax.Precision.HIGHEST, preferred_element_type=jnp.float32)
    moments = jnp.sum(mixed * table_ref[MOMENT : MOMENT + NB, :], axis=1, keepdims=True)
    column = jnp.broadcast_to(moments, (NB, CY))
    tiles = inv_ref.shape[1] // CY
    groups = tiles // 6
    out_ref[0, 0:1, :] = jnp.zeros((1, CY), jnp.float32)
    out_ref[groups - 1, WINDOW - 1 : WINDOW, :] = jnp.zeros((1, CY), jnp.float32)
    for t in range(tiles):
        total = jnp.sum(column * inv_ref[:, t * CY : (t + 1) * CY], axis=0, keepdims=True)
        for group in range(groups):
            place = t - (6 * group - 1)
            if 0 <= place < WINDOW:
                out_ref[group, place : place + 1, :] = total


def own_kernel(conc_ref, label_ref, out_ref, tail_ref, head_ref):
    for x in range(CX):
        for kind, values in enumerate((conc_ref[:, x, :], label_ref[:, x, :].astype(jnp.float32))):
            out_ref[kind, x] = values
            if x >= CX - FAR:
                tail_ref[kind, x - (CX - FAR)] = values
            if x < FAR:
                head_ref[kind, x] = values


def stage_kernel(_, scale_ref, slope_ref, inv_hbm, table_hbm, curve_ref, inv_ref, table_ref, sems):
    copies = [
        pltpu.make_async_copy(inv_hbm, inv_ref, sems.at[0]),
        pltpu.make_async_copy(table_hbm, table_ref, sems.at[1]),
    ]
    for copy in copies:
        copy.start()
    for n, ref in enumerate((scale_ref, slope_ref)):
        for k in range(8):
            curve_ref[8 * n + k : 8 * n + k + 1, :] = jnp.full((1, LANES), ref[k], jnp.float32)
    for copy in copies:
        copy.wait()


def pieces(refs):
    far_low, low, own, high, far_high = refs

    def at(kind, row):
        if row < FAR:
            return far_low[kind, row]
        if row < HALO:
            return low[kind, row - FAR]
        if row < HALO + CX:
            return own[kind, row - HALO]
        if row < HALO + 2 * CX:
            return high[kind, row - HALO - CX]
        return far_high[kind, row - HALO - 2 * CX]

    return at


def strip_kernel(far_low, low, own, high, far_high, up_ref, down_ref):
    at = pieces((far_low, low, own, high, far_high))
    for pack in range(PACKS):
        up = jnp.zeros((NZ, CY), jnp.float32)
        down = jnp.zeros((NZ, CY), jnp.float32)
        for slot in range(8):
            index = pack * 8 + slot
            if index < 2 * ROWS:
                values = at(index // ROWS, index % ROWS)
                mask = lanes_in((NZ, CY), (slot * STRIP, (slot + 1) * STRIP))
                up = jnp.where(mask, lane_shift(values, slot * STRIP - (CY - STRIP)), up)
                down = jnp.where(mask, lane_shift(values, slot * STRIP), down)
        up_ref[pack] = up
        down_ref[pack] = down


def setup_kernel(
    curve_ref, inv_ref, table_ref, far_low, low, own, high, far_high, left_ref, right_ref,
    west_out, south_out, below_out, inverse_out, source_out, out_ref,
    conc, label, coeff, line_ref,
):
    at = pieces((far_low, low, own, high, far_high))
    tile = (NZ, CY)
    m_right, m_right_own = lanes_in(tile, (16, 32)), lanes_in(tile, (0, 3))
    m_left, m_left_own = lanes_in(tile, (96, 112)), lanes_in(tile, (125, 128))
    m_end, m_start = lanes_in(tile, (13, 16)), lanes_in(tile, (112, 115))
    zero = jnp.zeros(tile, jnp.float32)
    for kind, target in ((0, conc), (1, label)):
        for row in range(ROWS):
            index = kind * ROWS + row
            values = at(kind, row)
            from_left, from_right = left_ref[index // 8], right_ref[index // 8]
            slot = (index % 8) * STRIP
            second = jnp.where(m_right, lane_shift(from_right, 16 - slot), zero)
            second = jnp.where(m_right_own, lane_shift(from_right, -slot), second)
            second = jnp.where(m_left, lane_shift(from_left, 96 - slot), second)
            second = jnp.where(m_left_own, lane_shift(from_left, 112 - slot), second)
            second = jnp.where(m_end, lane_shift(values, 16), second)
            second = jnp.where(m_start, lane_shift(values, -16), second)
            target[row, :, :CY] = values
            target[row, :, CY:] = second

    def diffusivity(row, _):
        kind = label[row].astype(jnp.int32) & 7
        bits = [(kind & (1 << b)) != 0 for b in range(3)]

        def pick(table):
            layer = [jnp.broadcast_to(curve_ref[table + k : table + k + 1, :], (NZ, LANES)) for k in range(8)]
            for bit in bits:
                layer = [jnp.where(bit, layer[2 * n + 1], layer[2 * n]) for n in range(len(layer) // 2)]
            return layer[0]

        coeff[row] = pick(0) * jnp.exp(pick(8) * conc[row])
        return 0

    lax.fori_loop(0, ROWS, diffusivity, 0)

    def pair(a, b, la, lb):
        weight = jnp.where(la == lb, 0.5, 0.5 * CONTACT)
        return jnp.where((la > 0.5) & (lb > 0.5), weight * (a + b), 0.0)

    not_bottom = lax.broadcasted_iota(jnp.int32, (NZ, LANES), 0) > 0
    west_out[0] = jnp.zeros((NZ, LANES), jnp.float32)

    def faces(row, _):
        a, la = coeff[row], label[row]

        @pl.when(row > 0)
        def _():
            west_out[row] = pair(a, coeff[row - 1], la, label[row - 1])

        south_out[row] = pair(a, lane_shift(a, 1), la, lane_shift(la, 1))
        below_out[row] = jnp.where(not_bottom, pair(a, depth_shift(a, 1), la, depth_shift(la, 1)), 0.0)
        return 0

    lax.fori_loop(0, ROWS, faces, 0)
    box = lanes_in((NZ, LANES), (0, 130), (142, 160), (224, 242), (254, 256))

    def operator(row, _):
        following = jnp.minimum(row + 1, ROWS - 1)
        before = jnp.maximum(row - 1, 0)
        west, east, south, below, c = west_out[row], west_out[following], south_out[row], below_out[row], conc[row]
        diagonal = INVERSE_STEP + west + east + south + lane_shift(south, -1) + below + depth_shift(below, -1)
        inverse_out[row] = jnp.where(box, 1.0 / diagonal, 0.0)
        flux = west * (c - conc[before]) - east * (conc[following] - c) + side_flux(c, south, below)
        source_out[row] = -flux
        return 0

    lax.fori_loop(0, ROWS, operator, 0)
    spread_moments(lambda x: source_out[HALO + x, :, :CY], table_ref, inv_ref, line_ref, out_ref)


def local_kernel(_, r_ref, west_ref, south_ref, below_ref, inverse_ref, out_ref, u_ref, q_ref, x_ref, *, wide):
    scaled, steps = chebyshev()
    plus = lanes_in((NZ, LANES), (253, 256), (141, 144))
    minus = lanes_in((NZ, LANES), (128, 131), (240, 243))
    for block in range(-2, 3):
        low, high = max(-wide, 8 * block), min(CX - 1 + wide, 8 * block + 7)
        if low > high:
            continue
        box_low, box_high = max(8 * block - OV, -HALO), min(8 * block + 7 + OV, CX - 1 + HALO)

        def start(row):
            if not box_low <= row <= box_high:
                return None
            return scaled * inverse_ref[row + HALO] * r_ref[row + HALO]

        for number, (keep, gain) in enumerate(steps):
            more = len(steps) - 1 - number
            first, last = max(low - more, box_low), min(high + more, box_high)

            def held(row):
                if not box_low <= row <= box_high:
                    return None
                return u_ref[row - box_low]

            fetch = start if number == 0 else held
            now, before = fetch(first), fetch(first - 1)
            flow = west_ref[first + HALO] * (now if before is None else now - before)
            for row in range(first, last + 1):
                following = fetch(row + 1)
                if row + 1 + HALO < ROWS:
                    gate = west_ref[row + 1 + HALO]
                    onward = gate * (-now if following is None else following - now)
                else:
                    onward = jnp.zeros_like(now)
                place = row - box_low
                applied = INVERSE_STEP * now + (flow - onward)
                applied = applied + side_flux(now, south_ref[row + HALO], below_ref[row + HALO])
                remain = (r_ref[row + HALO] if number == 0 else q_ref[place]) - applied
                step = keep * now + gain * (inverse_ref[row + HALO] * remain)
                result = (now if number == 0 else x_ref[place]) + step
                if more:
                    u_ref[place] = step
                    q_ref[place] = remain
                    x_ref[place] = result
                else:
                    merged = jnp.where(plus, lane_shift(result, 16), result)
                    out_ref[row + HALO] = jnp.where(minus, lane_shift(result, -16), merged)
                now, flow = following, onward


def turn_kernel(in_ref, out_ref):
    total = in_ref[0]
    for peer in range(1, in_ref.shape[0]):
        total = total + in_ref[peer]
    for z in range(N_Z):
        out_ref[z] = total[z // 2 : z // 2 + SPAN, :]


def answer_kernel(in_ref, out_ref):
    total = in_ref[0]
    for peer in range(1, N_Z):
        total = total + in_ref[peer]
    out_ref[...] = total


def coarse_rows(odd, answers, table_ref, flat_ref, wavy_ref):
    def weighted(answer):
        blocks = []
        for block in range(5):
            choice = []
            for index in (block, block + 1):
                row = jnp.broadcast_to(answer[index // 2 : index // 2 + 1, :], (CX, 2 * NB))
                choice.append(row * table_ref[HALF + (index % 2) * CX : HALF + (index % 2 + 1) * CX, :])
            blocks.append(jnp.where(odd, choice[1], choice[0]))
        return jnp.concatenate(blocks, axis=0)

    left, own, right = (weighted(a[...]) for a in answers)
    dot = functools.partial(jnp.dot, precision=lax.Precision.HIGHEST, preferred_element_type=jnp.float32)
    own_at = lambda n: dot(own, table_ref[OWN + n * CY : OWN + (n + 1) * CY, :])
    for s, target in enumerate((flat_ref, wavy_ref)):
        first = SIDE + s * 4 * NB
        beside = dot(left, table_ref[first : first + CY, :]) + dot(right, table_ref[first + CY : first + 2 * CY, :])
        target[:, :CY] = own_at(2 * s)
        target[:, CY:] = own_at(2 * s + 1) + beside


def update_kernel(*refs, reach, first):
    refs = list(refs)
    take = lambda count: [refs.pop(0) for _ in range(count)]
    odd_ref, left_ref, own_ref, right_ref = take(4)
    x_ref, source_ref, west_ref, south_ref, below_ref = take(5)
    (table_ref,) = take(1)
    (old_ref,) = take(0 if first else 1) or (None,)
    if reach:
        (inv_ref,) = take(1)
        u_ref, r_ref, out_ref = take(3)
        flat_ref, wavy_ref, line_ref = take(3)
    else:
        (packed_ref,) = take(1)
        updated_ref, residual_ref = take(2)
        flat_ref, wavy_ref = take(2)
        u_ref = None
    coarse_rows(odd_ref[0] == 1, (left_ref, own_ref, right_ref), table_ref, flat_ref, wavy_ref)
    wave = table_ref[WAVE : WAVE + NZ, :]
    wave = jnp.concatenate([wave, wave], axis=1)

    def fresh(row):
        place = row + 2 * CX
        field = jnp.broadcast_to(flat_ref[place : place + 1, :], (NZ, LANES))
        field = field + wave * jnp.broadcast_to(wavy_ref[place : place + 1, :], (NZ, LANES))
        value = x_ref[row + HALO] + field
        if not first:
            value = old_ref[row + HALO] + value
        if u_ref is not None:
            u_ref[row + HALO] = value
        return value

    before, now = fresh(-reach - 1), fresh(-reach)
    flow = west_ref[HALO - reach] * (now - before)
    for row in range(-reach, CX + reach):
        following = fresh(row + 1)
        onward = west_ref[row + 1 + HALO] * (following - now)
        applied = INVERSE_STEP * now + (flow - onward)
        applied = applied + side_flux(now, south_ref[row + HALO], below_ref[row + HALO])
        remain = source_ref[row + HALO] - applied
        if reach:
            r_ref[row + HALO] = remain
        else:
            updated_ref[:, row, :] = packed_ref[0, row] + now[:, :CY]
            residual_ref[:, row, :] = remain[:, :CY]
        now, flow = following, onward
    if reach:
        spread_moments(lambda x: r_ref[HALO + x, :, :CY], table_ref, inv_ref, line_ref, out_ref)


def vmem(count):
    return [pl.BlockSpec(memory_space=pltpu.VMEM)] * count


def shaped(*shape):
    return jax.ShapeDtypeStruct(shape, jnp.float32)


def moved(array, axis, by):
    size = lax.axis_size(axis)
    pairs = [(i, i + by) for i in range(size) if 0 <= i + by < size]
    return lax.ppermute(array, axis, pairs)


def room(mebibytes):
    return pltpu.CompilerParams(vmem_limit_bytes=mebibytes * 2**20)


def cost(flops):
    return pl.CostEstimate(flops=flops, bytes_accessed=4_000_000, transcendentals=0)


def on_device(concentration, labels, curve_scale, curve_slope, coarse_inv):
    size = lax.axis_size("gx")
    n_y = size // N_Z
    along_z = [[y * N_Z + z for z in range(N_Z)] for y in range(n_y)]
    along_y = [[y * N_Z + z for y in range(n_y)] for z in range(N_Z)]
    odd = (lax.axis_index("gx") & 1).astype(jnp.int32).reshape(1)
    odd, concentration = lax.optimization_barrier((odd, concentration))
    frame = shaped(ROWS, NZ, LANES)
    smem, anywhere = pl.BlockSpec(memory_space=pltpu.SMEM), pl.BlockSpec(memory_space=pl.ANY)
    hbm = pl.BlockSpec(memory_space=pltpu.HBM)
    scratch = lambda *shape: pltpu.VMEM(shape, jnp.float32)
    line_scratch = scratch(MZ * CX, CY)
    table_scratch = [scratch(5 * CX, LANES)] * 2

    own, tail, head = pl.pallas_call(
        own_kernel,
        out_shape=[shaped(2, CX, NZ, CY), shaped(2, FAR, NZ, CY), shaped(2, FAR, NZ, CY)],
        in_specs=vmem(2),
        out_specs=vmem(3),
        compiler_params=room(4),
        name="own",
    )(concentration, labels)
    low, high = moved(own, "gx", 1), moved(own, "gx", -1)
    far_low, far_high = moved(tail, "gx", 2), moved(head, "gx", -2)
    curve, inverse_rows, table = pl.pallas_call(
        stage_kernel,
        out_shape=[shaped(16, LANES), shaped(NB, NB * size), shaped(WAVE + NZ, CY)],
        in_specs=[anywhere, smem, smem, hbm, hbm],
        out_specs=vmem(3),
        scratch_shapes=[pltpu.SemaphoreType.DMA((2,))],
        compiler_params=room(4),
        cost_estimate=cost(1_000_000),
        name="stage",
    )(own, curve_scale, curve_slope, coarse_inv[0], jnp.asarray(tables()))
    parts = (far_low, low, own, high, far_high)
    up, down = pl.pallas_call(
        strip_kernel,
        out_shape=[shaped(PACKS, NZ, CY)] * 2,
        in_specs=vmem(5),
        out_specs=vmem(2),
        compiler_params=room(4),
        name="strips",
    )(*parts)
    left, right = moved(up, "gy", 1), moved(down, "gy", -1)
    west, south, below, inverse, source, partial = pl.pallas_call(
        setup_kernel,
        out_shape=[frame] * 5 + [shaped(n_y, WINDOW, CY)],
        in_specs=vmem(10),
        out_specs=vmem(6),
        scratch_shapes=[scratch(ROWS, NZ, LANES)] * 3 + [line_scratch],
        compiler_params=room(8),
        name="setup",
    )(curve, inverse_rows, table, *parts, left, right)

    residual, update = source, None
    for sweep, reach in enumerate(REACH):
        through = lax.all_to_all(partial, "gx", 0, 0, tiled=True, axis_index_groups=along_y)
        turned = pl.pallas_call(
            turn_kernel,
            out_shape=shaped(N_Z, SPAN, CY),
            in_specs=vmem(1),
            out_specs=vmem(1)[0],
            compiler_params=room(4),
            name="turn",
        )(through)
        arrived = lax.all_to_all(turned, "gx", 0, 0, tiled=True, axis_index_groups=along_z)
        answer = pl.pallas_call(
            answer_kernel,
            out_shape=shaped(SPAN, CY),
            in_specs=vmem(1),
            out_specs=vmem(1)[0],
            compiler_params=room(4),
            name="answer",
        )(arrived)
        answers = (moved(answer, "gy", 1), answer, moved(answer, "gy", -1))
        local = pl.pallas_call(
            functools.partial(local_kernel, wide=reach + 1),
            out_shape=frame,
            in_specs=[anywhere] + vmem(5),
            out_specs=vmem(1)[0],
            scratch_shapes=[scratch(CX + 2 * OV, NZ, LANES)] * 3,
            compiler_params=room(8),
            cost_estimate=cost(20_000_000),
            name="local",
        )(answer, residual, west, south, below, inverse)
        operands = [odd, *answers, local, source, west, south, below, table]
        operands += [] if sweep == 0 else [update]
        kernel = functools.partial(update_kernel, reach=reach, first=sweep == 0)
        if reach:
            operands += [inverse_rows]
            update, residual, partial = pl.pallas_call(
                kernel,
                out_shape=[frame, frame, shaped(n_y, WINDOW, CY)],
                in_specs=[smem] + vmem(len(operands) - 1),
                out_specs=vmem(3),
                scratch_shapes=table_scratch + [line_scratch],
                compiler_params=room(8),
                name="update",
            )(*operands)
        else:
            operands += [own]
            return pl.pallas_call(
                kernel,
                out_shape=[shaped(NZ, CX, CY)] * 2,
                in_specs=[smem] + vmem(len(operands) - 1),
                out_specs=vmem(2),
                scratch_shapes=table_scratch,
                compiler_params=room(8),
                name="final",
            )(*operands)


def solution(mesh):
    return jax.shard_map(
        on_device,
        mesh=mesh,
        in_specs=(P(None, "gx", "gy"), P(None, "gx", "gy"), P(), P(), P("gy", "gx", None)),
        out_specs=(P(None, "gx", "gy"), P(None, "gx", "gy")),
        check_vma=False,
    )
```

```python
import functools
import math

import jax
import jax.numpy as jnp
import numpy as np
from jax import lax
from jax.experimental import pallas as pl
from jax.experimental.pallas import tpu as pltpu
from jax.sharding import PartitionSpec as P

NZ = 16
CX = 8
CY = 128
OV = 2
SWEEPS = 3
CHEB = 4
MZ = 2
MX = 4
MY = 8
NB = 64
N_Z = 12
INVERSE_STEP = 0.004
CONTACT = 0.3
LOWER_BOUND = 0.1
UPPER_BOUND = 1.9

HALO = 13
ROWS = CX + 2 * HALO
FAR = HALO - CX
LANES = 256
STRIP = 16
WINDOW = 8
SPAN = 3
REACH = (8, 4, 0)
PACKS = 9


def cosine_table(mode_count, length):
    position = np.arange(length) + 0.5
    order = np.arange(mode_count)
    scaling = np.where(order == 0, math.sqrt(1.0 / length), math.sqrt(2.0 / length))
    return scaling[:, None] * np.cos(math.pi * order[:, None] * position[None, :] / length)


def tables():
    depth, first, second = cosine_table(MZ, NZ), cosine_table(MX, CX), cosine_table(MY, CY)
    flat = depth[0, 0]
    mix = np.zeros((NB, MZ * CX))
    rows = np.zeros((NB, CY))
    for s in range(MZ):
        for p in range(MX):
            for q in range(MY):
                n = (s * MX + p) * MY + q
                mix[n, s * CX : (s + 1) * CX] = first[p] * (flat if s == 0 else 1.0)
                rows[n] = second[q]
    half = np.zeros((2, CX, 2 * NB))
    spread = np.zeros((2 * NB, MZ, CY))
    for h in range(2):
        for s in range(MZ):
            for p in range(MX):
                for q in range(MY):
                    n = h * NB + (s * MX + p) * MY + q
                    half[h, :, n] = first[p]
                    spread[n, s] = second[q] * (flat if s == 0 else 1.0)
    own = np.zeros((2 * NB, MZ, LANES))
    own[:, :, :CY] = spread
    own[:, :, CY + 13 : CY + 16] = spread[:, :, 125:128]
    own[:, :, CY + 112 : CY + 115] = spread[:, :, 0:3]
    side = np.zeros((2, 2 * NB, MZ, CY))
    side[0, :, :, 96:112] = spread[:, :, 112:128]
    side[0, :, :, 125:128] = spread[:, :, 125:128]
    side[1, :, :, 16:32] = spread[:, :, 0:16]
    side[1, :, :, 0:3] = spread[:, :, 0:3]
    wave = np.broadcast_to(depth[1][:, None], (NZ, CY))
    mix = np.pad(mix, ((0, 0), (0, CY - MZ * CX)))
    parts = [own[:, s, k * CY : (k + 1) * CY] for s in range(MZ) for k in range(2)]
    parts += [side[:, :, s].reshape(4 * NB, CY) for s in range(MZ)]
    parts += [rows, mix, half.reshape(2 * CX, 2 * NB), wave]
    return np.concatenate(parts, axis=0).astype(np.float32)


OWN, SIDE, MOMENT, MIX, HALF, WAVE = 0, 512, 1024, 1088, 1152, 1168


def lane_shift(values, by):
    return pltpu.roll(values, by % values.shape[-1], axis=values.ndim - 1)


def depth_shift(values, by):
    return pltpu.roll(values, by % NZ, axis=0)


def lanes_in(shape, *ranges):
    lane = lax.broadcasted_iota(jnp.int32, shape, len(shape) - 1)
    inside = jnp.zeros(shape, jnp.bool_)
    for low, high in ranges:
        inside = inside | ((lane >= low) & (lane < high))
    return inside


def chebyshev():
    centre = (UPPER_BOUND + LOWER_BOUND) / 2.0
    radius = (UPPER_BOUND - LOWER_BOUND) / 2.0
    spread = centre / radius
    ratio = 1.0 / spread
    steps = []
    for _ in range(CHEB - 1):
        following = 1.0 / (2.0 * spread - ratio)
        steps.append((following * ratio, 2.0 * following / radius))
        ratio = following
    return 1.0 / centre, steps


def side_flux(values, south, below):
    across = south * (values - lane_shift(values, 1))
    upward = below * (values - depth_shift(values, 1))
    return (across - lane_shift(across, -1)) + (upward - depth_shift(upward, -1))


def spread_moments(r_row, table_ref, inv_ref, line_ref, out_ref):
    for x in range(CX):
        row = r_row(x)
        line_ref[x : x + 1, :] = jnp.sum(row, axis=0, keepdims=True)
        line_ref[CX + x : CX + x + 1, :] = jnp.sum(row * table_ref[WAVE : WAVE + NZ, :], axis=0, keepdims=True)
    mix = table_ref[MIX : MIX + NB, : MZ * CX]
    mixed = jnp.dot(mix, line_ref[...], precision=lax.Precision.HIGHEST, preferred_element_type=jnp.float32)
    moments = jnp.sum(mixed * table_ref[MOMENT : MOMENT + NB, :], axis=1, keepdims=True)
    column = jnp.broadcast_to(moments, (NB, CY))
    tiles = inv_ref.shape[1] // CY
    groups = tiles // 6
    out_ref[0, 0:1, :] = jnp.zeros((1, CY), jnp.float32)
    out_ref[groups - 1, WINDOW - 1 : WINDOW, :] = jnp.zeros((1, CY), jnp.float32)
    for t in range(tiles):
        total = jnp.sum(column * inv_ref[:, t * CY : (t + 1) * CY], axis=0, keepdims=True)
        for group in range(groups):
            place = t - (6 * group - 1)
            if 0 <= place < WINDOW:
                out_ref[group, place : place + 1, :] = total


def own_kernel(conc_ref, label_ref, out_ref, tail_ref, head_ref):
    for x in range(CX):
        for kind, values in enumerate((conc_ref[:, x, :], label_ref[:, x, :].astype(jnp.float32))):
            out_ref[kind, x] = values
            if x >= CX - FAR:
                tail_ref[kind, x - (CX - FAR)] = values
            if x < FAR:
                head_ref[kind, x] = values


def stage_kernel(_, scale_ref, slope_ref, inv_hbm, table_hbm, curve_ref, inv_ref, table_ref, sems):
    copies = [
        pltpu.make_async_copy(inv_hbm, inv_ref, sems.at[0]),
        pltpu.make_async_copy(table_hbm, table_ref, sems.at[1]),
    ]
    for copy in copies:
        copy.start()
    for n, ref in enumerate((scale_ref, slope_ref)):
        for k in range(8):
            curve_ref[8 * n + k : 8 * n + k + 1, :] = jnp.full((1, CY), ref[k], jnp.float32)
    for copy in copies:
        copy.wait()


def pieces(refs):
    far_low, low, own, high, far_high = refs

    def at(kind, row):
        if row < FAR:
            return far_low[kind, row]
        if row < HALO:
            return low[kind, row - FAR]
        if row < HALO + CX:
            return own[kind, row - HALO]
        if row < HALO + 2 * CX:
            return high[kind, row - HALO - CX]
        return far_high[kind, row - HALO - 2 * CX]

    return at


def strip_kernel(_, far_low, low, own, high, far_high, up_ref, down_ref):
    at = pieces((far_low, low, own, high, far_high))
    for pack in range(PACKS):
        up = jnp.zeros((NZ, CY), jnp.float32)
        down = jnp.zeros((NZ, CY), jnp.float32)
        for slot in range(8):
            index = pack * 8 + slot
            if index < 2 * ROWS:
                values = at(index // ROWS, index % ROWS)
                mask = lanes_in((NZ, CY), (slot * STRIP, (slot + 1) * STRIP))
                up = jnp.where(mask, lane_shift(values, slot * STRIP - (CY - STRIP)), up)
                down = jnp.where(mask, lane_shift(values, slot * STRIP), down)
        up_ref[pack] = up
        down_ref[pack] = down


class Beside:
    def __init__(self, first, second):
        self.first, self.second = first, second

    def __getitem__(self, row):
        return jnp.concatenate([self.first[row], self.second[row]], axis=1)


def rows_in_pairs(step):
    def both(pair, _):
        step(2 * pair)
        step(2 * pair + 1)
        return 0

    lax.fori_loop(0, ROWS // 2, both, 0)


def diffusivity(conc, label, curve_ref):
    kind = label.astype(jnp.int32) & 7
    bits = [(kind & (1 << b)) != 0 for b in range(3)]

    def pick(table):
        layer = [jnp.broadcast_to(curve_ref[table + k : table + k + 1, :], conc.shape) for k in range(8)]
        for bit in bits:
            layer = [jnp.where(bit, layer[2 * n + 1], layer[2 * n]) for n in range(len(layer) // 2)]
        return layer[0]

    return pick(0) * jnp.exp(pick(8) * conc)


def pair_weight(a, b, la, lb):
    weight = jnp.where(la == lb, 0.5, 0.5 * CONTACT)
    return jnp.where(jnp.minimum(la, lb) > 0.5, weight * (a + b), 0.0)


def tile_faces(row, coeff, label, west, below):
    a, la = coeff[row], label[row]
    before = jnp.maximum(row - 1, 0)
    west[row] = pair_weight(a, coeff[before], la, label[before])
    not_bottom = lax.broadcasted_iota(jnp.int32, a.shape, 0) > 0
    below[row] = jnp.where(not_bottom, pair_weight(a, depth_shift(a, 1), la, depth_shift(la, 1)), 0.0)


def tile_kernel(curve_ref, far_low, low, own, high, far_high, conc, label, coeff, west, below):
    at = pieces((far_low, low, own, high, far_high))
    for row in range(ROWS):
        conc[row] = at(0, row)
        label[row] = at(1, row)

    def fill(row):
        coeff[row] = diffusivity(conc[row], label[row], curve_ref)

    rows_in_pairs(fill)
    rows_in_pairs(lambda row: tile_faces(row, coeff, label, west, below))


def setup_kernel(
    curve_ref, inv_ref, table_ref, conc0, label0, coeff0, west0, below0, left_ref, right_ref,
    west1, below1, south_out, inverse_out, source_out, out_ref,
    conc1, label1, coeff1, line_ref,
):
    tile = (NZ, CY)
    m_right, m_right_own = lanes_in(tile, (16, 32)), lanes_in(tile, (0, 3))
    m_left, m_left_own = lanes_in(tile, (96, 112)), lanes_in(tile, (125, 128))
    m_end, m_start = lanes_in(tile, (13, 16)), lanes_in(tile, (112, 115))
    zero = jnp.zeros(tile, jnp.float32)
    for pack in range(PACKS):
        from_left, from_right = left_ref[pack], right_ref[pack]
        for part in range(8):
            index = pack * 8 + part
            if index >= 2 * ROWS:
                continue
            kind, row = index // ROWS, index % ROWS
            first, second = ((conc0, conc1), (label0, label1))[kind]
            values, slot = first[row], part * STRIP
            merged = jnp.where(m_right, lane_shift(from_right, 16 - slot), zero)
            merged = jnp.where(m_right_own, lane_shift(from_right, -slot), merged)
            merged = jnp.where(m_left, lane_shift(from_left, 96 - slot), merged)
            merged = jnp.where(m_left_own, lane_shift(from_left, 112 - slot), merged)
            merged = jnp.where(m_end, lane_shift(values, 16), merged)
            second[row] = jnp.where(m_start, lane_shift(values, -16), merged)

    def fill(row):
        coeff1[row] = diffusivity(conc1[row], label1[row], curve_ref)

    rows_in_pairs(fill)
    coeff, label, conc = Beside(coeff0, coeff1), Beside(label0, label1), Beside(conc0, conc1)

    def faces(row):
        tile_faces(row, coeff1, label1, west1, below1)
        a, la = coeff[row], label[row]
        south_out[row] = pair_weight(a, lane_shift(a, 1), la, lane_shift(la, 1))

    rows_in_pairs(faces)
    west_all, below_all = Beside(west0, west1), Beside(below0, below1)
    box = lanes_in((NZ, LANES), (0, 130), (142, 160), (224, 242), (254, 256))

    def operator(row):
        following = jnp.minimum(row + 1, ROWS - 1)
        before = jnp.maximum(row - 1, 0)
        west, east, south, below = west_all[row], west_all[following], south_out[row], below_all[row]
        c = conc[row]
        diagonal = INVERSE_STEP + west + east + south + lane_shift(south, -1) + below + depth_shift(below, -1)
        inverse_out[row] = jnp.where(box, 1.0 / diagonal, 0.0)
        flux = east * (conc[following] - c) - west * (c - conc[before])
        source_out[row] = flux - side_flux(c, south, below)

    rows_in_pairs(operator)
    spread_moments(lambda x: source_out[HALO + x, :, :CY], table_ref, inv_ref, line_ref, out_ref)


def local_kernel(
    _, r_ref, west0, west1, south_ref, below0, below1, inverse_ref, out_ref, u_ref, q_ref, x_ref, *, wide
):
    west_ref, below_ref = Beside(west0, west1), Beside(below0, below1)
    scaled, steps = chebyshev()
    plus = lanes_in((NZ, LANES), (253, 256), (141, 144))
    minus = lanes_in((NZ, LANES), (128, 131), (240, 243))

    def solve(base, low, high, box_low, box_high, limit):
        def start(row):
            if not box_low <= row <= box_high:
                return None
            return scaled * inverse_ref[base + row] * r_ref[base + row]

        def held(row):
            if not box_low <= row <= box_high:
                return None
            return u_ref[row - box_low]

        for number, (keep, gain) in enumerate(steps):
            more = len(steps) - 1 - number
            first, last = max(low - more, box_low), min(high + more, box_high)
            fetch = start if number == 0 else held
            now, before = fetch(first), fetch(first - 1)
            flow = west_ref[base + first] * (now if before is None else now - before)
            for row in range(first, last + 1):
                following = fetch(row + 1)
                if row + 1 < limit:
                    gate = west_ref[base + row + 1]
                    onward = gate * (-now if following is None else following - now)
                else:
                    onward = jnp.zeros_like(now)
                place = row - box_low
                applied = INVERSE_STEP * now + (flow - onward)
                applied = applied + side_flux(now, south_ref[base + row], below_ref[base + row])
                remain = (r_ref[base + row] if number == 0 else q_ref[place]) - applied
                step = keep * now + gain * (inverse_ref[base + row] * remain)
                if more:
                    u_ref[place] = step
                    q_ref[place] = remain
                if low <= row <= high:
                    result = (now if number == 0 else x_ref[place]) + step
                    if more:
                        x_ref[place] = result
                    else:
                        merged = jnp.where(plus, lane_shift(result, 16), result)
                        out_ref[base + row] = jnp.where(minus, lane_shift(result, -16), merged)
                now, flow = following, onward

    whole = [block for block in range(-2, 3) if -wide <= 8 * block and 8 * block + 7 <= CX - 1 + wide]
    for block in range(-2, 3):
        low, high = max(-wide, 8 * block), min(CX - 1 + wide, 8 * block + 7)
        if low > high or (block in whole and len(whole) > 1):
            continue
        base = HALO + 8 * block
        box_low, box_high = max(8 * block - OV, -HALO), min(8 * block + 7 + OV, CX - 1 + HALO)
        at = lambda row: row - 8 * block
        solve(base, at(low), at(high), at(box_low), at(box_high), ROWS - base)
    if len(whole) > 1:

        def body(number, _):
            solve(HALO + 8 * (number + whole[0]), 0, CX - 1, -OV, CX - 1 + OV, CX + OV + 1)
            return 0

        lax.fori_loop(0, len(whole), body, 0)


def turn_kernel(in_ref, out_ref):
    total = in_ref[0]
    for peer in range(1, in_ref.shape[0]):
        total = total + in_ref[peer]
    for z in range(N_Z):
        out_ref[z] = total[z // 2 : z // 2 + SPAN, :]


def answer_kernel(in_ref, out_ref):
    total = in_ref[0]
    for peer in range(1, N_Z):
        total = total + in_ref[peer]
    out_ref[...] = total


def coarse_rows(odd, answers, table_ref, flat_ref, wavy_ref):
    def weighted(answer):
        blocks = []
        for block in range(5):
            choice = []
            for index in (block, block + 1):
                row = jnp.broadcast_to(answer[index // 2 : index // 2 + 1, :], (CX, 2 * NB))
                choice.append(row * table_ref[HALF + (index % 2) * CX : HALF + (index % 2 + 1) * CX, :])
            blocks.append(jnp.where(odd, choice[1], choice[0]))
        return jnp.concatenate(blocks, axis=0)

    left, own, right = (weighted(a[...]) for a in answers)
    dot = functools.partial(jnp.dot, precision=lax.Precision.HIGHEST, preferred_element_type=jnp.float32)
    own_at = lambda n: dot(own, table_ref[OWN + n * CY : OWN + (n + 1) * CY, :])
    for s, target in enumerate((flat_ref, wavy_ref)):
        first = SIDE + s * 4 * NB
        beside = dot(left, table_ref[first : first + CY, :]) + dot(right, table_ref[first + CY : first + 2 * CY, :])
        target[:, :CY] = own_at(2 * s)
        target[:, CY:] = own_at(2 * s + 1) + beside


def update_kernel(*refs, reach, first):
    refs = list(refs)
    take = lambda count: [refs.pop(0) for _ in range(count)]
    odd_ref, left_ref, own_ref, right_ref = take(4)
    x_ref, source_ref, west0, west1, south_ref, below0, below1 = take(7)
    west_ref, below_ref = Beside(west0, west1), Beside(below0, below1)
    (table_ref,) = take(1)
    (old_ref,) = take(0 if first else 1) or (None,)
    if reach:
        (inv_ref,) = take(1)
        u_ref, r_ref, out_ref = take(3)
        flat_ref, wavy_ref, line_ref = take(3)
    else:
        (packed_ref,) = take(1)
        updated_ref, residual_ref = take(2)
        flat_ref, wavy_ref = take(2)
        u_ref = None
    coarse_rows(odd_ref[0] == 1, (left_ref, own_ref, right_ref), table_ref, flat_ref, wavy_ref)
    wave = table_ref[WAVE : WAVE + NZ, :]
    wave = jnp.concatenate([wave, wave], axis=1)

    def fresh(row):
        place = row + 2 * CX
        field = jnp.broadcast_to(flat_ref[place : place + 1, :], (NZ, LANES))
        field = field + wave * jnp.broadcast_to(wavy_ref[place : place + 1, :], (NZ, LANES))
        value = x_ref[row + HALO] + field
        if not first:
            value = old_ref[row + HALO] + value
        if u_ref is not None:
            u_ref[row + HALO] = value
        return value

    before, now = fresh(-reach - 1), fresh(-reach)
    flow = west_ref[HALO - reach] * (now - before)
    for row in range(-reach, CX + reach):
        following = fresh(row + 1)
        onward = west_ref[row + 1 + HALO] * (following - now)
        applied = INVERSE_STEP * now + (flow - onward)
        applied = applied + side_flux(now, south_ref[row + HALO], below_ref[row + HALO])
        remain = source_ref[row + HALO] - applied
        if reach:
            r_ref[row + HALO] = remain
        else:
            updated_ref[:, row, :] = packed_ref[0, row] + now[:, :CY]
            residual_ref[:, row, :] = remain[:, :CY]
        now, flow = following, onward
    if reach:
        spread_moments(lambda x: r_ref[HALO + x, :, :CY], table_ref, inv_ref, line_ref, out_ref)


def vmem(count):
    return [pl.BlockSpec(memory_space=pltpu.VMEM)] * count


def shaped(*shape):
    return jax.ShapeDtypeStruct(shape, jnp.float32)


def moved(array, axis, by):
    size = lax.axis_size(axis)
    pairs = [(i, i + by) for i in range(size) if 0 <= i + by < size]
    return lax.ppermute(array, axis, pairs)


def room(mebibytes):
    return pltpu.CompilerParams(vmem_limit_bytes=mebibytes * 2**20)


def cost(flops):
    return pl.CostEstimate(flops=flops, bytes_accessed=4_000_000, transcendentals=0)


def on_device(concentration, labels, curve_scale, curve_slope, coarse_inv):
    size = lax.axis_size("gx")
    n_y = size // N_Z
    along_z = [[y * N_Z + z for z in range(N_Z)] for y in range(n_y)]
    along_y = [[y * N_Z + z for y in range(n_y)] for z in range(N_Z)]
    odd = (lax.axis_index("gx") & 1).astype(jnp.int32).reshape(1)
    odd, concentration = lax.optimization_barrier((odd, concentration))
    frame = shaped(ROWS, NZ, LANES)
    smem, anywhere = pl.BlockSpec(memory_space=pltpu.SMEM), pl.BlockSpec(memory_space=pl.ANY)
    hbm = pl.BlockSpec(memory_space=pltpu.HBM)
    scratch = lambda *shape: pltpu.VMEM(shape, jnp.float32)
    line_scratch = scratch(MZ * CX, CY)
    table_scratch = [scratch(5 * CX, LANES)] * 2

    own, tail, head = pl.pallas_call(
        own_kernel,
        out_shape=[shaped(2, CX, NZ, CY), shaped(2, FAR, NZ, CY), shaped(2, FAR, NZ, CY)],
        in_specs=vmem(2),
        out_specs=vmem(3),
        compiler_params=room(4),
        name="own",
    )(concentration, labels)
    low, high = moved(own, "gx", 1), moved(own, "gx", -1)
    far_low, far_high = moved(tail, "gx", 2), moved(head, "gx", -2)
    curve, inverse_rows, table = pl.pallas_call(
        stage_kernel,
        out_shape=[shaped(16, CY), shaped(NB, NB * size), shaped(WAVE + NZ, CY)],
        in_specs=[anywhere, smem, smem, hbm, hbm],
        out_specs=vmem(3),
        scratch_shapes=[pltpu.SemaphoreType.DMA((2,))],
        compiler_params=room(4),
        cost_estimate=cost(1_000_000),
        name="stage",
    )(own, curve_scale, curve_slope, coarse_inv[0], jnp.asarray(tables()))
    parts = (far_low, low, own, high, far_high)
    up, down = pl.pallas_call(
        strip_kernel,
        out_shape=[shaped(PACKS, NZ, CY)] * 2,
        in_specs=[anywhere] + vmem(5),
        out_specs=vmem(2),
        compiler_params=room(4),
        name="strips",
    )(curve, *parts)
    left, right = moved(up, "gy", 1), moved(down, "gy", -1)
    half_frame = shaped(ROWS, NZ, CY)
    tiled = pl.pallas_call(
        tile_kernel,
        out_shape=[half_frame] * 5,
        in_specs=vmem(6),
        out_specs=vmem(5),
        compiler_params=room(4),
        cost_estimate=cost(10_000_000),
        name="tile",
    )(curve, *parts)
    west0, below0 = tiled[3:]
    west1, below1, south, inverse, source, partial = pl.pallas_call(
        setup_kernel,
        out_shape=[half_frame] * 2 + [frame] * 3 + [shaped(n_y, WINDOW, CY)],
        in_specs=vmem(10),
        out_specs=vmem(6),
        scratch_shapes=[scratch(ROWS, NZ, CY)] * 3 + [line_scratch],
        compiler_params=room(8),
        name="setup",
    )(curve, inverse_rows, table, *tiled, left, right)
    faces = (west0, west1, south, below0, below1)

    residual, update = source, None
    for sweep, reach in enumerate(REACH):
        through = lax.all_to_all(partial, "gx", 0, 0, tiled=True, axis_index_groups=along_y)
        turned = pl.pallas_call(
            turn_kernel,
            out_shape=shaped(N_Z, SPAN, CY),
            in_specs=vmem(1),
            out_specs=vmem(1)[0],
            compiler_params=room(4),
            name="turn",
        )(through)
        arrived = lax.all_to_all(turned, "gx", 0, 0, tiled=True, axis_index_groups=along_z)
        answer = pl.pallas_call(
            answer_kernel,
            out_shape=shaped(SPAN, CY),
            in_specs=vmem(1),
            out_specs=vmem(1)[0],
            compiler_params=room(4),
            name="answer",
        )(arrived)
        answers = (moved(answer, "gy", 1), answer, moved(answer, "gy", -1))
        local = pl.pallas_call(
            functools.partial(local_kernel, wide=reach + 1),
            out_shape=frame,
            in_specs=[anywhere] + vmem(7),
            out_specs=vmem(1)[0],
            scratch_shapes=[scratch(CX + 2 * OV, NZ, LANES)] * 3,
            compiler_params=room(8),
            cost_estimate=cost(20_000_000),
            name="local",
        )(answer, residual, *faces, inverse)
        operands = [odd, *answers, local, source, *faces, table]
        operands += [] if sweep == 0 else [update]
        kernel = functools.partial(update_kernel, reach=reach, first=sweep == 0)
        if reach:
            operands += [inverse_rows]
            update, residual, partial = pl.pallas_call(
                kernel,
                out_shape=[frame, frame, shaped(n_y, WINDOW, CY)],
                in_specs=[smem] + vmem(len(operands) - 1),
                out_specs=vmem(3),
                scratch_shapes=table_scratch + [line_scratch],
                compiler_params=room(8),
                name="update",
            )(*operands)
        else:
            operands += [own]
            return pl.pallas_call(
                kernel,
                out_shape=[shaped(NZ, CX, CY)] * 2,
                in_specs=[smem] + vmem(len(operands) - 1),
                out_specs=vmem(2),
                scratch_shapes=table_scratch,
                compiler_params=room(8),
                name="final",
            )(*operands)


def solution(mesh):
    return jax.shard_map(
        on_device,
        mesh=mesh,
        in_specs=(P(None, "gx", "gy"), P(None, "gx", "gy"), P(), P(), P("gy", "gx", None)),
        out_specs=(P(None, "gx", "gy"), P(None, "gx", "gy")),
        check_vma=False,
    )
```

```python
import functools
import math

import jax
import jax.numpy as jnp
import numpy as np
from jax import lax
from jax.experimental import pallas as pl
from jax.experimental.pallas import tpu as pltpu
from jax.sharding import PartitionSpec as P

NZ = 16
CX = 8
CY = 128
OV = 2
SWEEPS = 3
CHEB = 4
MZ = 2
MX = 4
MY = 8
NB = 64
N_Z = 12
INVERSE_STEP = 0.004
CONTACT = 0.3
LOWER_BOUND = 0.1
UPPER_BOUND = 1.9

HALO = 13
ROWS = CX + 2 * HALO
FAR = HALO - CX
LANES = 256
STRIP = 16
WINDOW = 8
SPAN = 3
REACH = (8, 4, 0)
PACKS = 9


def cosine_table(mode_count, length):
    position = np.arange(length) + 0.5
    order = np.arange(mode_count)
    scaling = np.where(order == 0, math.sqrt(1.0 / length), math.sqrt(2.0 / length))
    return scaling[:, None] * np.cos(math.pi * order[:, None] * position[None, :] / length)


def tables():
    depth, first, second = cosine_table(MZ, NZ), cosine_table(MX, CX), cosine_table(MY, CY)
    flat = depth[0, 0]
    mix = np.zeros((NB, MZ * CX))
    rows = np.zeros((NB, CY))
    for s in range(MZ):
        for p in range(MX):
            for q in range(MY):
                n = (s * MX + p) * MY + q
                mix[n, s * CX : (s + 1) * CX] = first[p] * (flat if s == 0 else 1.0)
                rows[n] = second[q]
    half = np.zeros((2, CX, 2 * NB))
    spread = np.zeros((2 * NB, MZ, CY))
    for h in range(2):
        for s in range(MZ):
            for p in range(MX):
                for q in range(MY):
                    n = h * NB + (s * MX + p) * MY + q
                    half[h, :, n] = first[p]
                    spread[n, s] = second[q] * (flat if s == 0 else 1.0)
    own = np.zeros((2 * NB, MZ, LANES))
    own[:, :, :CY] = spread
    own[:, :, CY + 13 : CY + 16] = spread[:, :, 125:128]
    own[:, :, CY + 112 : CY + 115] = spread[:, :, 0:3]
    side = np.zeros((2, 2 * NB, MZ, CY))
    side[0, :, :, 96:112] = spread[:, :, 112:128]
    side[0, :, :, 125:128] = spread[:, :, 125:128]
    side[1, :, :, 16:32] = spread[:, :, 0:16]
    side[1, :, :, 0:3] = spread[:, :, 0:3]
    wave = np.broadcast_to(depth[1][:, None], (NZ, CY))
    mix = np.pad(mix, ((0, 0), (0, CY - MZ * CX)))
    parts = [own[:, s, k * CY : (k + 1) * CY] for s in range(MZ) for k in range(2)]
    parts += [side[:, :, s].reshape(4 * NB, CY) for s in range(MZ)]
    parts += [rows, mix, half.reshape(2 * CX, 2 * NB), wave]
    return np.concatenate(parts, axis=0).astype(np.float32)


OWN, SIDE, MOMENT, MIX, HALF, WAVE = 0, 512, 1024, 1088, 1152, 1168


def lane_shift(values, by):
    return pltpu.roll(values, by % values.shape[-1], axis=values.ndim - 1)


def depth_shift(values, by):
    return pltpu.roll(values, by % NZ, axis=0)


def lanes_in(shape, *ranges):
    lane = lax.broadcasted_iota(jnp.int32, shape, len(shape) - 1)
    inside = jnp.zeros(shape, jnp.bool_)
    for low, high in ranges:
        inside = inside | ((lane >= low) & (lane < high))
    return inside


def chebyshev():
    centre = (UPPER_BOUND + LOWER_BOUND) / 2.0
    radius = (UPPER_BOUND - LOWER_BOUND) / 2.0
    spread = centre / radius
    ratio = 1.0 / spread
    steps = []
    for _ in range(CHEB - 1):
        following = 1.0 / (2.0 * spread - ratio)
        steps.append((following * ratio, 2.0 * following / radius))
        ratio = following
    return 1.0 / centre, steps


def side_flux(values, south, below):
    across = south * (values - lane_shift(values, 1))
    upward = below * (values - depth_shift(values, 1))
    return (across - lane_shift(across, -1)) + (upward - depth_shift(upward, -1))


def spread_moments(r_row, table_ref, inv_ref, line_ref, out_ref):
    for x in range(CX):
        row = r_row(x)
        line_ref[x : x + 1, :] = jnp.sum(row, axis=0, keepdims=True)
        line_ref[CX + x : CX + x + 1, :] = jnp.sum(row * table_ref[WAVE : WAVE + NZ, :], axis=0, keepdims=True)
    mix = table_ref[MIX : MIX + NB, : MZ * CX]
    mixed = jnp.dot(mix, line_ref[...], precision=lax.Precision.HIGHEST, preferred_element_type=jnp.float32)
    moments = jnp.sum(mixed * table_ref[MOMENT : MOMENT + NB, :], axis=1, keepdims=True)
    column = jnp.broadcast_to(moments, (NB, CY))
    tiles = inv_ref.shape[1] // CY
    groups = tiles // 6
    out_ref[0, 0:1, :] = jnp.zeros((1, CY), jnp.float32)
    out_ref[groups - 1, WINDOW - 1 : WINDOW, :] = jnp.zeros((1, CY), jnp.float32)
    for t in range(tiles):
        total = jnp.sum(column * inv_ref[:, t * CY : (t + 1) * CY], axis=0, keepdims=True)
        for group in range(groups):
            place = t - (6 * group - 1)
            if 0 <= place < WINDOW:
                out_ref[group, place : place + 1, :] = total


def own_kernel(place_ref, conc_ref, label_ref, out_ref, one_ref, two_ref):
    upper = bit(place_ref, 4)
    for x in range(CX):
        for kind, values in enumerate((conc_ref[:, x, :], label_ref[:, x, :].astype(jnp.float32))):
            out_ref[kind, x] = values
    for kind in range(2):
        for row in range(FAR):
            head, tail = out_ref[kind, row], out_ref[kind, CX - FAR + row]
            one_ref[kind, row] = jnp.where(upper, head, tail)
            two_ref[kind, row] = jnp.where(upper, tail, head)


def stage_kernel(_, scale_ref, slope_ref, inv_hbm, table_hbm, curve_ref, inv_ref, table_ref, sems):
    copies = [
        pltpu.make_async_copy(inv_hbm, inv_ref, sems.at[0]),
        pltpu.make_async_copy(table_hbm, table_ref, sems.at[1]),
    ]
    for copy in copies:
        copy.start()
    for n, ref in enumerate((scale_ref, slope_ref)):
        for k in range(8):
            curve_ref[8 * n + k : 8 * n + k + 1, :] = jnp.full((1, CY), ref[k], jnp.float32)
    for copy in copies:
        copy.wait()


def bit(place_ref, which):
    return ((place_ref[0] >> which) & 1) == 1


def pieces(place_ref, refs):
    near_one, near_two, far_one, far_two, own = refs
    odd, upper = bit(place_ref, 3), bit(place_ref, 4)

    def at(kind, row):
        if HALO <= row < HALO + CX:
            return own[kind, row - HALO]
        below = row < HALO
        if FAR <= row < HALO + 2 * CX:
            place = row - FAR if below else row - HALO - CX
            flag, one, two = odd, near_one, near_two
        else:
            place = row if below else row - HALO - 2 * CX
            flag, one, two = upper, far_one, far_two
        first, second = one[kind, place], two[kind, place]
        return jnp.where(flag, first, second) if below else jnp.where(flag, second, first)

    return at


def strip_kernel(place_ref, _, near_one, near_two, far_one, far_two, own, one_ref, two_ref):
    at = pieces(place_ref, (near_one, near_two, far_one, far_two, own))
    odd = bit(place_ref, 0)
    for pack in range(PACKS):
        up = jnp.zeros((NZ, CY), jnp.float32)
        down = jnp.zeros((NZ, CY), jnp.float32)
        for slot in range(8):
            index = pack * 8 + slot
            if index < 2 * ROWS:
                values = at(index // ROWS, index % ROWS)
                mask = lanes_in((NZ, CY), (slot * STRIP, (slot + 1) * STRIP))
                up = jnp.where(mask, lane_shift(values, slot * STRIP - (CY - STRIP)), up)
                down = jnp.where(mask, lane_shift(values, slot * STRIP), down)
        one_ref[pack] = jnp.where(odd, down, up)
        two_ref[pack] = jnp.where(odd, up, down)


class Beside:
    def __init__(self, first, second):
        self.first, self.second = first, second

    def __getitem__(self, row):
        return jnp.concatenate([self.first[row], self.second[row]], axis=1)


def rows_in_pairs(step):
    def both(pair, _):
        step(2 * pair)
        step(2 * pair + 1)
        return 0

    lax.fori_loop(0, ROWS // 2, both, 0)


def diffusivity(conc, label, curve_ref):
    kind = label.astype(jnp.int32) & 7
    bits = [(kind & (1 << b)) != 0 for b in range(3)]

    def pick(table):
        layer = [jnp.broadcast_to(curve_ref[table + k : table + k + 1, :], conc.shape) for k in range(8)]
        for bit in bits:
            layer = [jnp.where(bit, layer[2 * n + 1], layer[2 * n]) for n in range(len(layer) // 2)]
        return layer[0]

    return pick(0) * jnp.exp(pick(8) * conc)


def pair_weight(a, b, la, lb):
    weight = jnp.where(la == lb, 0.5, 0.5 * CONTACT)
    return jnp.where(jnp.minimum(la, lb) > 0.5, weight * (a + b), 0.0)


def tile_faces(row, coeff, label, west, below):
    a, la = coeff[row], label[row]
    before = jnp.maximum(row - 1, 0)
    west[row] = pair_weight(a, coeff[before], la, label[before])
    not_bottom = lax.broadcasted_iota(jnp.int32, a.shape, 0) > 0
    below[row] = jnp.where(not_bottom, pair_weight(a, depth_shift(a, 1), la, depth_shift(la, 1)), 0.0)


def tile_kernel(place_ref, curve_ref, near_one, near_two, far_one, far_two, own, conc, label, coeff, west, below):
    at = pieces(place_ref, (near_one, near_two, far_one, far_two, own))
    for row in range(ROWS):
        conc[row] = at(0, row)
        label[row] = at(1, row)

    def fill(row):
        coeff[row] = diffusivity(conc[row], label[row], curve_ref)

    rows_in_pairs(fill)
    rows_in_pairs(lambda row: tile_faces(row, coeff, label, west, below))


def setup_kernel(
    place_ref, curve_ref, inv_ref, table_ref, conc0, label0, coeff0, west0, below0, one_ref, two_ref,
    west1, below1, south_out, inverse_out, source_out, out_ref,
    conc1, label1, coeff1, line_ref,
):
    tile = (NZ, CY)
    m_right, m_right_own = lanes_in(tile, (16, 32)), lanes_in(tile, (0, 3))
    m_left, m_left_own = lanes_in(tile, (96, 112)), lanes_in(tile, (125, 128))
    m_end, m_start = lanes_in(tile, (13, 16)), lanes_in(tile, (112, 115))
    zero = jnp.zeros(tile, jnp.float32)
    odd = bit(place_ref, 0)
    for pack in range(PACKS):
        one, two = one_ref[pack], two_ref[pack]
        from_left, from_right = jnp.where(odd, one, two), jnp.where(odd, two, one)
        for part in range(8):
            index = pack * 8 + part
            if index >= 2 * ROWS:
                continue
            kind, row = index // ROWS, index % ROWS
            first, second = ((conc0, conc1), (label0, label1))[kind]
            values, slot = first[row], part * STRIP
            merged = jnp.where(m_right, lane_shift(from_right, 16 - slot), zero)
            merged = jnp.where(m_right_own, lane_shift(from_right, -slot), merged)
            merged = jnp.where(m_left, lane_shift(from_left, 96 - slot), merged)
            merged = jnp.where(m_left_own, lane_shift(from_left, 112 - slot), merged)
            merged = jnp.where(m_end, lane_shift(values, 16), merged)
            second[row] = jnp.where(m_start, lane_shift(values, -16), merged)

    def fill(row):
        coeff1[row] = diffusivity(conc1[row], label1[row], curve_ref)

    rows_in_pairs(fill)
    coeff, label, conc = Beside(coeff0, coeff1), Beside(label0, label1), Beside(conc0, conc1)

    def faces(row):
        tile_faces(row, coeff1, label1, west1, below1)
        a, la = coeff[row], label[row]
        south_out[row] = pair_weight(a, lane_shift(a, 1), la, lane_shift(la, 1))

    rows_in_pairs(faces)
    west_all, below_all = Beside(west0, west1), Beside(below0, below1)
    box = lanes_in((NZ, LANES), (0, 130), (142, 160), (224, 242), (254, 256))

    def operator(row):
        following = jnp.minimum(row + 1, ROWS - 1)
        before = jnp.maximum(row - 1, 0)
        west, east, south, below = west_all[row], west_all[following], south_out[row], below_all[row]
        c = conc[row]
        diagonal = INVERSE_STEP + west + east + south + lane_shift(south, -1) + below + depth_shift(below, -1)
        inverse_out[row] = jnp.where(box, 1.0 / diagonal, 0.0)
        flux = east * (conc[following] - c) - west * (c - conc[before])
        source_out[row] = flux - side_flux(c, south, below)

    rows_in_pairs(operator)
    spread_moments(lambda x: source_out[HALO + x, :, :CY], table_ref, inv_ref, line_ref, out_ref)


def local_kernel(
    _, r_ref, west0, west1, south_ref, below0, below1, inverse_ref, out_ref, u_ref, q_ref, x_ref, *, wide
):
    west_ref, below_ref = Beside(west0, west1), Beside(below0, below1)
    scaled, steps = chebyshev()
    plus = lanes_in((NZ, LANES), (253, 256), (141, 144))
    minus = lanes_in((NZ, LANES), (128, 131), (240, 243))

    def solve(base, low, high, box_low, box_high, limit):
        def start(row):
            if not box_low <= row <= box_high:
                return None
            return scaled * inverse_ref[base + row] * r_ref[base + row]

        def held(row):
            if not box_low <= row <= box_high:
                return None
            return u_ref[row - box_low]

        for number, (keep, gain) in enumerate(steps):
            more = len(steps) - 1 - number
            first, last = max(low - more, box_low), min(high + more, box_high)
            fetch = start if number == 0 else held
            now, before = fetch(first), fetch(first - 1)
            flow = west_ref[base + first] * (now if before is None else now - before)
            for row in range(first, last + 1):
                following = fetch(row + 1)
                if row + 1 < limit:
                    gate = west_ref[base + row + 1]
                    onward = gate * (-now if following is None else following - now)
                else:
                    onward = jnp.zeros_like(now)
                place = row - box_low
                applied = INVERSE_STEP * now + (flow - onward)
                applied = applied + side_flux(now, south_ref[base + row], below_ref[base + row])
                remain = (r_ref[base + row] if number == 0 else q_ref[place]) - applied
                step = keep * now + gain * (inverse_ref[base + row] * remain)
                if more:
                    u_ref[place] = step
                    q_ref[place] = remain
                if low <= row <= high:
                    result = (now if number == 0 else x_ref[place]) + step
                    if more:
                        x_ref[place] = result
                    else:
                        merged = jnp.where(plus, lane_shift(result, 16), result)
                        out_ref[base + row] = jnp.where(minus, lane_shift(result, -16), merged)
                now, flow = following, onward

    whole = [-1, 0, 1] if wide >= 5 else []
    for block in range(-2, 3):
        low, high = max(-wide, 8 * block), min(CX - 1 + wide, 8 * block + 7)
        if low > high or block in whole:
            continue
        base = HALO + 8 * block
        box_low, box_high = max(8 * block - OV, -HALO), min(8 * block + 7 + OV, CX - 1 + HALO)
        at = lambda row: row - 8 * block
        solve(base, at(low), at(high), at(box_low), at(box_high), ROWS - base)
    if whole:

        def body(number, _):
            solve(HALO + 8 * (number + whole[0]), 0, CX - 1, -OV, CX - 1 + OV, CX + OV + 1)
            return 0

        lax.fori_loop(0, len(whole), body, 0)


def turn_kernel(in_ref, out_ref):
    total = in_ref[0]
    for peer in range(1, in_ref.shape[0]):
        total = total + in_ref[peer]
    for z in range(N_Z):
        out_ref[z] = total[z // 2 : z // 2 + SPAN, :]


def answer_kernel(in_ref, out_ref):
    total = in_ref[0]
    for peer in range(1, N_Z):
        total = total + in_ref[peer]
    out_ref[...] = total


def coarse_rows(odd, answers, table_ref, flat_ref, wavy_ref):
    def weighted(answer):
        blocks = []
        for block in range(5):
            choice = []
            for index in (block, block + 1):
                row = jnp.broadcast_to(answer[index // 2 : index // 2 + 1, :], (CX, 2 * NB))
                choice.append(row * table_ref[HALF + (index % 2) * CX : HALF + (index % 2 + 1) * CX, :])
            blocks.append(jnp.where(odd, choice[1], choice[0]))
        return jnp.concatenate(blocks, axis=0)

    left, own, right = (weighted(a) for a in answers)
    dot = functools.partial(jnp.dot, precision=lax.Precision.HIGHEST, preferred_element_type=jnp.float32)
    own_at = lambda n: dot(own, table_ref[OWN + n * CY : OWN + (n + 1) * CY, :])
    for s, target in enumerate((flat_ref, wavy_ref)):
        first = SIDE + s * 4 * NB
        beside = dot(left, table_ref[first : first + CY, :]) + dot(right, table_ref[first + CY : first + 2 * CY, :])
        target[:, :CY] = own_at(2 * s)
        target[:, CY:] = own_at(2 * s + 1) + beside


def update_kernel(*refs, reach, first):
    refs = list(refs)
    take = lambda count: [refs.pop(0) for _ in range(count)]
    place_ref, one_ref, own_ref, two_ref = take(4)
    right_column = bit(place_ref, 0)
    one, two = one_ref[...], two_ref[...]
    answers = (jnp.where(right_column, one, two), own_ref[...], jnp.where(right_column, two, one))
    x_ref, source_ref, west0, west1, south_ref, below0, below1 = take(7)
    west_ref, below_ref = Beside(west0, west1), Beside(below0, below1)
    (table_ref,) = take(1)
    (old_ref,) = take(0 if first else 1) or (None,)
    if reach:
        (inv_ref,) = take(1)
        u_ref, r_ref, out_ref = take(3)
        flat_ref, wavy_ref, line_ref = take(3)
    else:
        (packed_ref,) = take(1)
        updated_ref, residual_ref = take(2)
        flat_ref, wavy_ref = take(2)
        u_ref = None
    coarse_rows(bit(place_ref, 3), answers, table_ref, flat_ref, wavy_ref)
    wave = table_ref[WAVE : WAVE + NZ, :]
    wave = jnp.concatenate([wave, wave], axis=1)

    def fresh(row):
        place = row + 2 * CX
        field = jnp.broadcast_to(flat_ref[place : place + 1, :], (NZ, LANES))
        field = field + wave * jnp.broadcast_to(wavy_ref[place : place + 1, :], (NZ, LANES))
        value = x_ref[row + HALO] + field
        if not first:
            value = old_ref[row + HALO] + value
        if u_ref is not None:
            u_ref[row + HALO] = value
        return value

    if reach:
        for row in (-reach - 2, -reach - 1, CX + reach, CX + reach + 1):
            r_ref[row + HALO] = jnp.zeros((NZ, LANES), jnp.float32)
    before, now = fresh(-reach - 1), fresh(-reach)
    flow = west_ref[HALO - reach] * (now - before)
    for row in range(-reach, CX + reach):
        following = fresh(row + 1)
        onward = west_ref[row + 1 + HALO] * (following - now)
        applied = INVERSE_STEP * now + (flow - onward)
        applied = applied + side_flux(now, south_ref[row + HALO], below_ref[row + HALO])
        remain = source_ref[row + HALO] - applied
        if reach:
            r_ref[row + HALO] = remain
        else:
            updated_ref[:, row, :] = packed_ref[0, row] + now[:, :CY]
            residual_ref[:, row, :] = remain[:, :CY]
        now, flow = following, onward
    if reach:
        spread_moments(lambda x: r_ref[HALO + x, :, :CY], table_ref, inv_ref, line_ref, out_ref)


def vmem(count):
    return [pl.BlockSpec(memory_space=pltpu.VMEM)] * count


def shaped(*shape):
    return jax.ShapeDtypeStruct(shape, jnp.float32)


def swapped(array, axis, apart):
    size = lax.axis_size(axis)
    arrays = array if isinstance(array, (list, tuple)) else (array, array)
    results = []
    for offset, values in zip((0, apart), arrays):
        pairs = []
        for low in range(size - apart):
            if (low - offset) % (2 * apart) < apart:
                pairs += [(low, low + apart), (low + apart, low)]
        results.append(lax.ppermute(values, axis, pairs))
    return results


def room(mebibytes):
    return pltpu.CompilerParams(vmem_limit_bytes=mebibytes * 2**20)


def cost(flops):
    return pl.CostEstimate(flops=flops, bytes_accessed=4_000_000, transcendentals=0)


def on_device(concentration, labels, curve_scale, curve_slope, coarse_inv):
    size = lax.axis_size("gx")
    n_y = size // N_Z
    along_z = [[y * N_Z + z for z in range(N_Z)] for y in range(n_y)]
    along_y = [[y * N_Z + z for y in range(n_y)] for z in range(N_Z)]
    place = (8 * lax.axis_index("gx") + lax.axis_index("gy")).astype(jnp.int32).reshape(1)
    place, concentration = lax.optimization_barrier((place, concentration))
    frame = shaped(ROWS, NZ, LANES)
    smem, anywhere = pl.BlockSpec(memory_space=pltpu.SMEM), pl.BlockSpec(memory_space=pl.ANY)
    hbm = pl.BlockSpec(memory_space=pltpu.HBM)
    scratch = lambda *shape: pltpu.VMEM(shape, jnp.float32)
    line_scratch = scratch(MZ * CX, CY)
    table_scratch = [scratch(5 * CX, LANES)] * 2

    own, far_one, far_two = pl.pallas_call(
        own_kernel,
        out_shape=[shaped(2, CX, NZ, CY), shaped(2, FAR, NZ, CY), shaped(2, FAR, NZ, CY)],
        in_specs=[smem] + vmem(2),
        out_specs=vmem(3),
        compiler_params=room(4),
        name="own",
    )(place, concentration, labels)
    parts = (*swapped(own, "gx", 1), *swapped((far_one, far_two), "gx", 2), own)
    curve, inverse_rows, table = pl.pallas_call(
        stage_kernel,
        out_shape=[shaped(16, CY), shaped(NB, NB * size), shaped(WAVE + NZ, CY)],
        in_specs=[anywhere, smem, smem, hbm, hbm],
        out_specs=vmem(3),
        scratch_shapes=[pltpu.SemaphoreType.DMA((2,))],
        compiler_params=room(4),
        cost_estimate=cost(1_000_000),
        name="stage",
    )(own, curve_scale, curve_slope, coarse_inv[0], jnp.asarray(tables()))
    strips = pl.pallas_call(
        strip_kernel,
        out_shape=[shaped(PACKS, NZ, CY)] * 2,
        in_specs=[smem, anywhere] + vmem(5),
        out_specs=vmem(2),
        compiler_params=room(4),
        name="strips",
    )(place, curve, *parts)
    strips = swapped(strips, "gy", 1)
    half_frame = shaped(ROWS, NZ, CY)
    tiled = pl.pallas_call(
        tile_kernel,
        out_shape=[half_frame] * 5,
        in_specs=[smem] + vmem(6),
        out_specs=vmem(5),
        compiler_params=room(4),
        cost_estimate=cost(10_000_000),
        name="tile",
    )(place, curve, *parts)
    west0, below0 = tiled[3:]
    west1, below1, south, inverse, source, partial = pl.pallas_call(
        setup_kernel,
        out_shape=[half_frame] * 2 + [frame] * 3 + [shaped(n_y, WINDOW, CY)],
        in_specs=[smem] + vmem(10),
        out_specs=vmem(6),
        scratch_shapes=[scratch(ROWS, NZ, CY)] * 3 + [line_scratch],
        compiler_params=room(8),
        name="setup",
    )(place, curve, inverse_rows, table, *tiled, *strips)
    faces = (west0, west1, south, below0, below1)

    residual, update = source, None
    for sweep, reach in enumerate(REACH):
        through = lax.all_to_all(partial, "gx", 0, 0, tiled=True, axis_index_groups=along_y)
        turned = pl.pallas_call(
            turn_kernel,
            out_shape=shaped(N_Z, SPAN, CY),
            in_specs=vmem(1),
            out_specs=vmem(1)[0],
            compiler_params=room(4),
            name="turn",
        )(through)
        arrived = lax.all_to_all(turned, "gx", 0, 0, tiled=True, axis_index_groups=along_z)
        answer = pl.pallas_call(
            answer_kernel,
            out_shape=shaped(SPAN, CY),
            in_specs=vmem(1),
            out_specs=vmem(1)[0],
            compiler_params=room(4),
            name="answer",
        )(arrived)
        one, two = swapped(answer, "gy", 1)
        local = pl.pallas_call(
            functools.partial(local_kernel, wide=reach + 1),
            out_shape=frame,
            in_specs=[anywhere] + vmem(7),
            out_specs=vmem(1)[0],
            scratch_shapes=[scratch(CX + 2 * OV, NZ, LANES)] * 3,
            compiler_params=room(8),
            cost_estimate=cost(20_000_000),
            name="local",
        )(answer, residual, *faces, inverse)
        operands = [place, one, answer, two, local, source, *faces, table]
        operands += [] if sweep == 0 else [update]
        kernel = functools.partial(update_kernel, reach=reach, first=sweep == 0)
        if reach:
            operands += [inverse_rows]
            update, residual, partial = pl.pallas_call(
                kernel,
                out_shape=[frame, frame, shaped(n_y, WINDOW, CY)],
                in_specs=[smem] + vmem(len(operands) - 1),
                out_specs=vmem(3),
                scratch_shapes=table_scratch + [line_scratch],
                compiler_params=room(8),
                name="update",
            )(*operands)
        else:
            operands += [own]
            return pl.pallas_call(
                kernel,
                out_shape=[shaped(NZ, CX, CY)] * 2,
                in_specs=[smem] + vmem(len(operands) - 1),
                out_specs=vmem(2),
                scratch_shapes=table_scratch,
                compiler_params=room(8),
                name="final",
            )(*operands)


def solution(mesh):
    return jax.shard_map(
        on_device,
        mesh=mesh,
        in_specs=(P(None, "gx", "gy"), P(None, "gx", "gy"), P(), P(), P("gy", "gx", None)),
        out_specs=(P(None, "gx", "gy"), P(None, "gx", "gy")),
        check_vma=False,
    )
```

```python
import functools
import math

import jax
import jax.numpy as jnp
import numpy as np
from jax import lax
from jax.experimental import pallas as pl
from jax.experimental.pallas import tpu as pltpu
from jax.sharding import PartitionSpec as P

NZ = 16
CX = 8
CY = 128
OV = 2
SWEEPS = 3
CHEB = 4
MZ = 2
MX = 4
MY = 8
NB = 64
N_Z = 12
INVERSE_STEP = 0.004
CONTACT = 0.3
LOWER_BOUND = 0.1
UPPER_BOUND = 1.9

HALO = 13
ROWS = CX + 2 * HALO
FAR = HALO - CX
LANES = 256
STRIP = 16
WINDOW = 8
SPAN = 3
REACH = (8, 4, 0)
PACKS = 9


def cosine_table(mode_count, length):
    position = np.arange(length) + 0.5
    order = np.arange(mode_count)
    scaling = np.where(order == 0, math.sqrt(1.0 / length), math.sqrt(2.0 / length))
    return scaling[:, None] * np.cos(math.pi * order[:, None] * position[None, :] / length)


def tables():
    depth, first, second = cosine_table(MZ, NZ), cosine_table(MX, CX), cosine_table(MY, CY)
    flat = depth[0, 0]
    mix = np.zeros((NB, MZ * CX))
    rows = np.zeros((NB, CY))
    for s in range(MZ):
        for p in range(MX):
            for q in range(MY):
                n = (s * MX + p) * MY + q
                mix[n, s * CX : (s + 1) * CX] = first[p] * (flat if s == 0 else 1.0)
                rows[n] = second[q]
    half = np.zeros((2, CX, 2 * NB))
    spread = np.zeros((2 * NB, MZ, CY))
    for h in range(2):
        for s in range(MZ):
            for p in range(MX):
                for q in range(MY):
                    n = h * NB + (s * MX + p) * MY + q
                    half[h, :, n] = first[p]
                    spread[n, s] = second[q] * (flat if s == 0 else 1.0)
    own = np.zeros((2 * NB, MZ, LANES))
    own[:, :, :CY] = spread
    own[:, :, CY + 13 : CY + 16] = spread[:, :, 125:128]
    own[:, :, CY + 112 : CY + 115] = spread[:, :, 0:3]
    side = np.zeros((2, 2 * NB, MZ, CY))
    side[0, :, :, 96:112] = spread[:, :, 112:128]
    side[0, :, :, 125:128] = spread[:, :, 125:128]
    side[1, :, :, 16:32] = spread[:, :, 0:16]
    side[1, :, :, 0:3] = spread[:, :, 0:3]
    wave = np.broadcast_to(depth[1][:, None], (NZ, CY))
    mix = np.pad(mix, ((0, 0), (0, CY - MZ * CX)))
    parts = [own[:, s, k * CY : (k + 1) * CY] for s in range(MZ) for k in range(2)]
    parts += [side[:, :, s].reshape(4 * NB, CY) for s in range(MZ)]
    parts += [rows, mix, half.reshape(2 * CX, 2 * NB), wave]
    return np.concatenate(parts, axis=0).astype(np.float32)


OWN, SIDE, MOMENT, MIX, HALF, WAVE = 0, 512, 1024, 1088, 1152, 1168


def lane_shift(values, by):
    return pltpu.roll(values, by % values.shape[-1], axis=values.ndim - 1)


def depth_shift(values, by):
    return pltpu.roll(values, by % NZ, axis=0)


def lanes_in(shape, *ranges):
    lane = lax.broadcasted_iota(jnp.int32, shape, len(shape) - 1)
    inside = jnp.zeros(shape, jnp.bool_)
    for low, high in ranges:
        inside = inside | ((lane >= low) & (lane < high))
    return inside


def chebyshev():
    centre = (UPPER_BOUND + LOWER_BOUND) / 2.0
    radius = (UPPER_BOUND - LOWER_BOUND) / 2.0
    spread = centre / radius
    ratio = 1.0 / spread
    steps = []
    for _ in range(CHEB - 1):
        following = 1.0 / (2.0 * spread - ratio)
        steps.append((following * ratio, 2.0 * following / radius))
        ratio = following
    return 1.0 / centre, steps


def side_flux(values, south, below):
    across = south * (values - lane_shift(values, 1))
    upward = below * (values - depth_shift(values, 1))
    return (across - lane_shift(across, -1)) + (upward - depth_shift(upward, -1))


def spread_moments(r_row, table_ref, inv_ref, line_ref, out_ref):
    for x in range(CX):
        row = r_row(x)
        line_ref[x : x + 1, :] = jnp.sum(row, axis=0, keepdims=True)
        line_ref[CX + x : CX + x + 1, :] = jnp.sum(row * table_ref[WAVE : WAVE + NZ, :], axis=0, keepdims=True)
    mix = table_ref[MIX : MIX + NB, : MZ * CX]
    mixed = jnp.dot(mix, line_ref[...], precision=lax.Precision.HIGHEST, preferred_element_type=jnp.float32)
    moments = jnp.sum(mixed * table_ref[MOMENT : MOMENT + NB, :], axis=1, keepdims=True)
    column = jnp.broadcast_to(moments, (NB, CY))
    tiles = inv_ref.shape[1] // CY
    groups = tiles // 6
    out_ref[0, 0:1, :] = jnp.zeros((1, CY), jnp.float32)
    out_ref[groups - 1, WINDOW - 1 : WINDOW, :] = jnp.zeros((1, CY), jnp.float32)
    for t in range(tiles):
        total = jnp.sum(column * inv_ref[:, t * CY : (t + 1) * CY], axis=0, keepdims=True)
        for group in range(groups):
            place = t - (6 * group - 1)
            if 0 <= place < WINDOW:
                out_ref[group, place : place + 1, :] = total


def bit(place_ref, which):
    return ((place_ref[0] >> which) & 1) == 1


def own_kernel(place_ref, conc_hbm, label_hbm, out_ref, one_ref, two_ref, conc_ref, label_ref, sems):
    copies = [
        pltpu.make_async_copy(conc_hbm, conc_ref, sems.at[0]),
        pltpu.make_async_copy(label_hbm, label_ref, sems.at[1]),
    ]
    for copy in copies:
        copy.start()
    upper = bit(place_ref, 4)
    for kind, copy in enumerate(copies):
        copy.wait()
        for x in range(CX):
            out_ref[kind, x] = conc_ref[:, x, :] if kind == 0 else label_ref[:, x, :].astype(jnp.float32)
    for kind in range(2):
        for row in range(FAR):
            head, tail = out_ref[kind, row], out_ref[kind, CX - FAR + row]
            one_ref[kind, row] = jnp.where(upper, head, tail)
            two_ref[kind, row] = jnp.where(upper, tail, head)


def curve_rows(scale_ref, slope_ref, curve_ref):
    for n, ref in enumerate((scale_ref, slope_ref)):
        for k in range(8):
            curve_ref[8 * n + k : 8 * n + k + 1, :] = jnp.full((1, CY), ref[k], jnp.float32)


def pieces(place_ref, refs):
    near_one, near_two, far_one, far_two, own = refs
    odd, upper = bit(place_ref, 3), bit(place_ref, 4)

    def at(kind, row):
        if HALO <= row < HALO + CX:
            return own[kind, row - HALO]
        below = row < HALO
        if FAR <= row < HALO + 2 * CX:
            place = row - FAR if below else row - HALO - CX
            flag, one, two = odd, near_one, near_two
        else:
            place = row if below else row - HALO - 2 * CX
            flag, one, two = upper, far_one, far_two
        first, second = one[kind, place], two[kind, place]
        return jnp.where(flag, first, second) if below else jnp.where(flag, second, first)

    return at


def strip_kernel(place_ref, near_one, near_two, far_one, far_two, own, one_ref, two_ref):
    at = pieces(place_ref, (near_one, near_two, far_one, far_two, own))
    odd = bit(place_ref, 0)
    for pack in range(PACKS):
        up = jnp.zeros((NZ, CY), jnp.float32)
        down = jnp.zeros((NZ, CY), jnp.float32)
        for slot in range(8):
            index = pack * 8 + slot
            if index < 2 * ROWS:
                values = at(index // ROWS, index % ROWS)
                mask = lanes_in((NZ, CY), (slot * STRIP, (slot + 1) * STRIP))
                up = jnp.where(mask, lane_shift(values, slot * STRIP - (CY - STRIP)), up)
                down = jnp.where(mask, lane_shift(values, slot * STRIP), down)
        one_ref[pack] = jnp.where(odd, down, up)
        two_ref[pack] = jnp.where(odd, up, down)


class Beside:
    def __init__(self, first, second):
        self.first, self.second = first, second

    def __getitem__(self, row):
        return jnp.concatenate([self.first[row], self.second[row]], axis=1)


def rows_in_pairs(step):
    def both(pair, _):
        step(2 * pair)
        step(2 * pair + 1)
        return 0

    lax.fori_loop(0, ROWS // 2, both, 0)


def diffusivity(conc, label, curve_ref):
    kind = label.astype(jnp.int32) & 7
    bits = [(kind & (1 << b)) != 0 for b in range(3)]

    def pick(table):
        layer = [jnp.broadcast_to(curve_ref[table + k : table + k + 1, :], conc.shape) for k in range(8)]
        for bit in bits:
            layer = [jnp.where(bit, layer[2 * n + 1], layer[2 * n]) for n in range(len(layer) // 2)]
        return layer[0]

    return pick(0) * jnp.exp(pick(8) * conc)


def pair_weight(a, b, la, lb):
    weight = jnp.where(la == lb, 0.5, 0.5 * CONTACT)
    return jnp.where(jnp.minimum(la, lb) > 0.5, weight * (a + b), 0.0)


def tile_faces(row, coeff, label, west, below):
    a, la = coeff[row], label[row]
    before = jnp.maximum(row - 1, 0)
    west[row] = pair_weight(a, coeff[before], la, label[before])
    not_bottom = lax.broadcasted_iota(jnp.int32, a.shape, 0) > 0
    below[row] = jnp.where(not_bottom, pair_weight(a, depth_shift(a, 1), la, depth_shift(la, 1)), 0.0)


def tile_sums(row, conc, west, below):
    following, before = jnp.minimum(row + 1, ROWS - 1), jnp.maximum(row - 1, 0)
    c, w, e, b = conc[row], west[row], west[following], below[row]
    upward = b * (c - depth_shift(c, 1))
    flux = e * (conc[following] - c) - w * (c - conc[before]) - (upward - depth_shift(upward, -1))
    return INVERSE_STEP + w + e + b + depth_shift(b, -1), flux


def tile_kernel(
    place_ref, scale_hbm, slope_hbm, inv_hbm, table_hbm, near_one, near_two, far_one, far_two, own,
    conc, label, coeff, west, below, diagonal, source, conc_edge, label_edge, curve_ref, inv_ref, table_ref,
    scale_ref, slope_ref, sems,
):
    sources = (scale_hbm, slope_hbm, inv_hbm, table_hbm)
    targets = (scale_ref, slope_ref, inv_ref, table_ref)
    copies = [pltpu.make_async_copy(a, b, sems.at[n]) for n, (a, b) in enumerate(zip(sources, targets))]
    for copy in copies:
        copy.start()
    at = pieces(place_ref, (near_one, near_two, far_one, far_two, own))
    end, start = lanes_in((NZ, CY), (13, 16)), lanes_in((NZ, CY), (112, 115))
    for kind, (target, edge) in enumerate(((conc, conc_edge), (label, label_edge))):
        for row in range(ROWS):
            values = at(kind, row)
            target[row] = values
            beside = jnp.where(end, lane_shift(values, 16), 0.0)
            edge[row] = jnp.where(start, lane_shift(values, -16), beside)
    copies[0].wait()
    copies[1].wait()
    curve_rows(scale_ref, slope_ref, curve_ref)

    def fill(row):
        coeff[row] = diffusivity(conc[row], label[row], curve_ref)

    rows_in_pairs(fill)
    rows_in_pairs(lambda row: tile_faces(row, coeff, label, west, below))

    def sums(row):
        diagonal[row], source[row] = tile_sums(row, conc, west, below)

    rows_in_pairs(sums)
    copies[2].wait()
    copies[3].wait()


def setup_kernel(
    place_ref,
    conc0, label0, coeff0, west0, below0, diagonal0, source0, conc_edge, label_edge, curve_ref, inv_ref, table_ref,
    one_ref, two_ref,
    west1, below1, south_out, inverse_out, source_out, out_ref,
    conc1, label1, coeff1, line_ref,
):
    tile = (NZ, CY)
    m_right, m_right_own = lanes_in(tile, (16, 32)), lanes_in(tile, (0, 3))
    m_left, m_left_own = lanes_in(tile, (96, 112)), lanes_in(tile, (125, 128))
    odd = bit(place_ref, 0)
    for pack in range(PACKS):
        one, two = one_ref[pack], two_ref[pack]
        from_left, from_right = jnp.where(odd, one, two), jnp.where(odd, two, one)
        for part in range(8):
            index = pack * 8 + part
            if index >= 2 * ROWS:
                continue
            kind, row = index // ROWS, index % ROWS
            edge, second = ((conc_edge, conc1), (label_edge, label1))[kind]
            slot = part * STRIP
            merged = jnp.where(m_right, lane_shift(from_right, 16 - slot), edge[row])
            merged = jnp.where(m_right_own, lane_shift(from_right, -slot), merged)
            merged = jnp.where(m_left, lane_shift(from_left, 96 - slot), merged)
            second[row] = jnp.where(m_left_own, lane_shift(from_left, 112 - slot), merged)

    def fill(row):
        coeff1[row] = diffusivity(conc1[row], label1[row], curve_ref)

    rows_in_pairs(fill)
    rows_in_pairs(lambda row: tile_faces(row, coeff1, label1, west1, below1))
    coeff, label, conc = Beside(coeff0, coeff1), Beside(label0, label1), Beside(conc0, conc1)
    box = lanes_in((NZ, LANES), (0, 130), (142, 160), (224, 242), (254, 256))

    def operator(row):
        a, la, c = coeff[row], label[row], conc[row]
        south = pair_weight(a, lane_shift(a, 1), la, lane_shift(la, 1))
        south_out[row] = south
        diagonal1, source1 = tile_sums(row, conc1, west1, below1)
        diagonal = jnp.concatenate([diagonal0[row], diagonal1], axis=1) + south + lane_shift(south, -1)
        inverse_out[row] = jnp.where(box, 1.0 / diagonal, 0.0)
        across = south * (c - lane_shift(c, 1))
        source_out[row] = jnp.concatenate([source0[row], source1], axis=1) - (across - lane_shift(across, -1))

    rows_in_pairs(operator)
    spread_moments(lambda x: source_out[HALO + x, :, :CY], table_ref, inv_ref, line_ref, out_ref)


def local_kernel(
    _, r_ref, west0, west1, south_ref, below0, below1, inverse_ref, out_ref, u_ref, q_ref, x_ref, *, wide
):
    west_ref, below_ref = Beside(west0, west1), Beside(below0, below1)
    scaled, steps = chebyshev()
    plus = lanes_in((NZ, LANES), (253, 256), (141, 144))
    minus = lanes_in((NZ, LANES), (128, 131), (240, 243))

    def solve(base, low, high, box_low, box_high, limit):
        def start(row):
            if not box_low <= row <= box_high:
                return None
            return scaled * inverse_ref[base + row] * r_ref[base + row]

        def held(row):
            if not box_low <= row <= box_high:
                return None
            return u_ref[row - box_low]

        for number, (keep, gain) in enumerate(steps):
            more = len(steps) - 1 - number
            first, last = max(low - more, box_low), min(high + more, box_high)
            fetch = start if number == 0 else held
            now, before = fetch(first), fetch(first - 1)
            flow = west_ref[base + first] * (now if before is None else now - before)
            for row in range(first, last + 1):
                following = fetch(row + 1)
                if row + 1 < limit:
                    gate = west_ref[base + row + 1]
                    onward = gate * (-now if following is None else following - now)
                else:
                    onward = jnp.zeros_like(now)
                place = row - box_low
                applied = INVERSE_STEP * now + (flow - onward)
                applied = applied + side_flux(now, south_ref[base + row], below_ref[base + row])
                remain = (r_ref[base + row] if number == 0 else q_ref[place]) - applied
                step = keep * now + gain * (inverse_ref[base + row] * remain)
                if more:
                    u_ref[place] = step
                    q_ref[place] = remain
                if low <= row <= high:
                    result = (now if number == 0 else x_ref[place]) + step
                    if more:
                        x_ref[place] = result
                    else:
                        merged = jnp.where(plus, lane_shift(result, 16), result)
                        out_ref[base + row] = jnp.where(minus, lane_shift(result, -16), merged)
                now, flow = following, onward

    whole = [-1, 0, 1] if wide >= 5 else []
    for block in range(-2, 3):
        low, high = max(-wide, 8 * block), min(CX - 1 + wide, 8 * block + 7)
        if low > high or block in whole:
            continue
        base = HALO + 8 * block
        box_low, box_high = max(8 * block - OV, -HALO), min(8 * block + 7 + OV, CX - 1 + HALO)
        at = lambda row: row - 8 * block
        solve(base, at(low), at(high), at(box_low), at(box_high), ROWS - base)
    if whole:

        def body(number, _):
            solve(HALO + 8 * (number + whole[0]), 0, CX - 1, -OV, CX - 1 + OV, CX + OV + 1)
            return 0

        lax.fori_loop(0, len(whole), body, 0)


def turn_kernel(in_ref, out_ref):
    total = in_ref[0]
    for peer in range(1, in_ref.shape[0]):
        total = total + in_ref[peer]
    for z in range(N_Z):
        out_ref[z] = total[z // 2 : z // 2 + SPAN, :]


def answer_kernel(in_ref, out_ref):
    total = in_ref[0]
    for peer in range(1, N_Z):
        total = total + in_ref[peer]
    out_ref[...] = total


def coarse_rows(odd, answers, table_ref, flat_ref, wavy_ref):
    def weighted(answer):
        blocks = []
        for block in range(5):
            choice = []
            for index in (block, block + 1):
                row = jnp.broadcast_to(answer[index // 2 : index // 2 + 1, :], (CX, 2 * NB))
                choice.append(row * table_ref[HALF + (index % 2) * CX : HALF + (index % 2 + 1) * CX, :])
            blocks.append(jnp.where(odd, choice[1], choice[0]))
        return jnp.concatenate(blocks, axis=0)

    left, own, right = (weighted(a) for a in answers)
    dot = functools.partial(jnp.dot, precision=lax.Precision.HIGHEST, preferred_element_type=jnp.float32)
    own_at = lambda n: dot(own, table_ref[OWN + n * CY : OWN + (n + 1) * CY, :])
    for s, target in enumerate((flat_ref, wavy_ref)):
        first = SIDE + s * 4 * NB
        beside = dot(left, table_ref[first : first + CY, :]) + dot(right, table_ref[first + CY : first + 2 * CY, :])
        target[:, :CY] = own_at(2 * s)
        target[:, CY:] = own_at(2 * s + 1) + beside


def update_kernel(*refs, reach, first):
    refs = list(refs)
    take = lambda count: [refs.pop(0) for _ in range(count)]
    place_ref, one_ref, own_ref, two_ref = take(4)
    right_column = bit(place_ref, 0)
    one, two = one_ref[...], two_ref[...]
    answers = (jnp.where(right_column, one, two), own_ref[...], jnp.where(right_column, two, one))
    x_ref, source_ref, west0, west1, south_ref, below0, below1 = take(7)
    west_ref, below_ref = Beside(west0, west1), Beside(below0, below1)
    (table_ref,) = take(1)
    (old_ref,) = take(0 if first else 1) or (None,)
    if reach:
        (inv_ref,) = take(1)
        u_ref, r_ref, out_ref = take(3)
        flat_ref, wavy_ref, line_ref = take(3)
    else:
        (packed_ref,) = take(1)
        updated_ref, residual_ref = take(2)
        flat_ref, wavy_ref = take(2)
        u_ref = None
    coarse_rows(bit(place_ref, 3), answers, table_ref, flat_ref, wavy_ref)
    wave = table_ref[WAVE : WAVE + NZ, :]
    wave = jnp.concatenate([wave, wave], axis=1)

    def fresh(row):
        place = row + 2 * CX
        field = jnp.broadcast_to(flat_ref[place : place + 1, :], (NZ, LANES))
        field = field + wave * jnp.broadcast_to(wavy_ref[place : place + 1, :], (NZ, LANES))
        value = x_ref[row + HALO] + field
        if not first:
            value = old_ref[row + HALO] + value
        if u_ref is not None:
            u_ref[row + HALO] = value
        return value

    if reach:
        for row in (-reach - 2, -reach - 1, CX + reach, CX + reach + 1):
            r_ref[row + HALO] = jnp.zeros((NZ, LANES), jnp.float32)
    before, now = fresh(-reach - 1), fresh(-reach)
    flow = west_ref[HALO - reach] * (now - before)
    for row in range(-reach, CX + reach):
        following = fresh(row + 1)
        onward = west_ref[row + 1 + HALO] * (following - now)
        applied = INVERSE_STEP * now + (flow - onward)
        applied = applied + side_flux(now, south_ref[row + HALO], below_ref[row + HALO])
        remain = source_ref[row + HALO] - applied
        if reach:
            r_ref[row + HALO] = remain
        else:
            updated_ref[:, row, :] = packed_ref[0, row] + now[:, :CY]
            residual_ref[:, row, :] = remain[:, :CY]
        now, flow = following, onward
    if reach:
        spread_moments(lambda x: r_ref[HALO + x, :, :CY], table_ref, inv_ref, line_ref, out_ref)


def vmem(count):
    return [pl.BlockSpec(memory_space=pltpu.VMEM)] * count


def shaped(*shape):
    return jax.ShapeDtypeStruct(shape, jnp.float32)


def swapped(array, axis, apart):
    size = lax.axis_size(axis)
    arrays = array if isinstance(array, (list, tuple)) else (array, array)
    results = []
    for offset, values in zip((0, apart), arrays):
        pairs = []
        for low in range(size - apart):
            if (low - offset) % (2 * apart) < apart:
                pairs += [(low, low + apart), (low + apart, low)]
        results.append(lax.ppermute(values, axis, pairs))
    return results


def room(mebibytes):
    return pltpu.CompilerParams(vmem_limit_bytes=mebibytes * 2**20)


def cost(flops, accessed=4_000_000):
    return pl.CostEstimate(flops=flops, bytes_accessed=accessed, transcendentals=0)


def on_device(concentration, labels, curve_scale, curve_slope, coarse_inv):
    size = lax.axis_size("gx")
    n_y = size // N_Z
    along_z = [[y * N_Z + z for z in range(N_Z)] for y in range(n_y)]
    along_y = [[y * N_Z + z for y in range(n_y)] for z in range(N_Z)]
    place = (8 * lax.axis_index("gx") + lax.axis_index("gy")).astype(jnp.int32).reshape(1)
    place, concentration = lax.optimization_barrier((place, concentration))
    frame = shaped(ROWS, NZ, LANES)
    smem, anywhere = pl.BlockSpec(memory_space=pltpu.SMEM), pl.BlockSpec(memory_space=pl.ANY)
    scratch = lambda *shape: pltpu.VMEM(shape, jnp.float32)
    line_scratch = scratch(MZ * CX, CY)
    table_scratch = [scratch(5 * CX, LANES)] * 2

    kept = lambda array: pltpu.with_memory_space_constraint(array, pltpu.HBM)
    hbm = pl.BlockSpec(memory_space=pltpu.HBM)
    own, *far = pl.pallas_call(
        own_kernel,
        out_shape=[shaped(2, CX, NZ, CY)] + [shaped(2, FAR, NZ, CY)] * 2,
        in_specs=[smem, hbm, hbm],
        out_specs=vmem(3),
        scratch_shapes=[scratch(NZ, CX, CY), pltpu.VMEM((NZ, CX, CY), jnp.int32), pltpu.SemaphoreType.DMA((2,))],
        compiler_params=room(4),
        name="own",
    )(place, kept(concentration), kept(labels))
    parts = (*swapped(own, "gx", 1), *swapped(far, "gx", 2), own)
    strips = pl.pallas_call(
        strip_kernel,
        out_shape=[shaped(PACKS, NZ, CY)] * 2,
        in_specs=[smem] + vmem(5),
        out_specs=vmem(2),
        compiler_params=room(4),
        name="strips",
    )(place, *parts)
    strips = swapped(strips, "gy", 1)
    half_frame = shaped(ROWS, NZ, CY)
    table = tables()
    tiled = pl.pallas_call(
        tile_kernel,
        out_shape=[half_frame] * 9 + [shaped(16, CY), shaped(NB, NB * size), shaped(*table.shape)],
        in_specs=[smem] + [hbm] * 4 + vmem(5),
        out_specs=vmem(12),
        scratch_shapes=[pltpu.SMEM((8,), jnp.float32)] * 2 + [pltpu.SemaphoreType.DMA((4,))],
        compiler_params=room(4),
        cost_estimate=cost(10_000_000),
        name="tile",
    )(place, *(kept(a) for a in (curve_scale, curve_slope, coarse_inv[0], jnp.asarray(table))), *parts)
    west0, below0 = tiled[3:5]
    inverse_rows, table = tiled[10:]
    west1, below1, south, inverse, source, partial = pl.pallas_call(
        setup_kernel,
        out_shape=[half_frame] * 2 + [frame] * 3 + [shaped(n_y, WINDOW, CY)],
        in_specs=[smem] + vmem(14),
        out_specs=vmem(6),
        scratch_shapes=[scratch(ROWS, NZ, CY)] * 3 + [line_scratch],
        compiler_params=room(8),
        name="setup",
    )(place, *tiled, *strips)
    faces = (west0, west1, south, below0, below1)

    residual, update = source, None
    for sweep, reach in enumerate(REACH):
        through = lax.all_to_all(partial, "gx", 0, 0, tiled=True, axis_index_groups=along_y)
        turned = pl.pallas_call(
            turn_kernel,
            out_shape=shaped(N_Z, SPAN, CY),
            in_specs=vmem(1),
            out_specs=vmem(1)[0],
            compiler_params=room(4),
            name="turn",
        )(through)
        arrived = lax.all_to_all(turned, "gx", 0, 0, tiled=True, axis_index_groups=along_z)
        answer = pl.pallas_call(
            answer_kernel,
            out_shape=shaped(SPAN, CY),
            in_specs=vmem(1),
            out_specs=vmem(1)[0],
            compiler_params=room(4),
            name="answer",
        )(arrived)
        one, two = swapped(answer, "gy", 1)
        local = pl.pallas_call(
            functools.partial(local_kernel, wide=reach + 1),
            out_shape=frame,
            in_specs=[anywhere] + vmem(7),
            out_specs=vmem(1)[0],
            scratch_shapes=[scratch(CX + 2 * OV, NZ, LANES)] * 3,
            compiler_params=room(8),
            cost_estimate=cost(20_000_000),
            name="local",
        )(answer, residual, *faces, inverse)
        operands = [place, one, answer, two, local, source, *faces, table]
        operands += [] if sweep == 0 else [update]
        kernel = functools.partial(update_kernel, reach=reach, first=sweep == 0)
        if reach:
            operands += [inverse_rows]
            update, residual, partial = pl.pallas_call(
                kernel,
                out_shape=[frame, frame, shaped(n_y, WINDOW, CY)],
                in_specs=[smem] + vmem(len(operands) - 1),
                out_specs=vmem(3),
                scratch_shapes=table_scratch + [line_scratch],
                compiler_params=room(8),
                name="update",
            )(*operands)
        else:
            operands += [own]
            return pl.pallas_call(
                kernel,
                out_shape=[shaped(NZ, CX, CY)] * 2,
                in_specs=[smem] + vmem(len(operands) - 1),
                out_specs=vmem(2),
                scratch_shapes=table_scratch,
                compiler_params=room(8),
                name="final",
            )(*operands)


def solution(mesh):
    return jax.shard_map(
        on_device,
        mesh=mesh,
        in_specs=(P(None, "gx", "gy"), P(None, "gx", "gy"), P(), P(), P("gy", "gx", None)),
        out_specs=(P(None, "gx", "gy"), P(None, "gx", "gy")),
        check_vma=False,
    )
```

```python
import functools
import math

import jax
import jax.numpy as jnp
import numpy as np
from jax import lax
from jax.experimental import pallas as pl
from jax.experimental.pallas import tpu as pltpu
from jax.sharding import PartitionSpec as P

NZ = 16
CX = 8
CY = 128
OV = 2
SWEEPS = 3
CHEB = 4
MZ = 2
MX = 4
MY = 8
NB = 64
N_Z = 12
INVERSE_STEP = 0.004
CONTACT = 0.3
LOWER_BOUND = 0.1
UPPER_BOUND = 1.9

HALO = 13
ROWS = CX + 2 * HALO
FAR = HALO - CX
LANES = 256
STRIP = 16
WINDOW = 8
SPAN = 3
REACH = (8, 4, 0)
PACKS = 9


def cosine_table(mode_count, length):
    position = np.arange(length) + 0.5
    order = np.arange(mode_count)
    scaling = np.where(order == 0, math.sqrt(1.0 / length), math.sqrt(2.0 / length))
    return scaling[:, None] * np.cos(math.pi * order[:, None] * position[None, :] / length)


def tables():
    depth, first, second = cosine_table(MZ, NZ), cosine_table(MX, CX), cosine_table(MY, CY)
    flat = depth[0, 0]
    mix = np.zeros((NB, MZ * CX))
    rows = np.zeros((NB, CY))
    for s in range(MZ):
        for p in range(MX):
            for q in range(MY):
                n = (s * MX + p) * MY + q
                mix[n, s * CX : (s + 1) * CX] = first[p] * (flat if s == 0 else 1.0)
                rows[n] = second[q]
    near = np.zeros((CX, NB))
    spread = np.zeros((NB, MZ, CY))
    for s in range(MZ):
        for p in range(MX):
            for q in range(MY):
                n = (s * MX + p) * MY + q
                near[:, n] = first[p]
                spread[n, s] = second[q] * (flat if s == 0 else 1.0)
    own = np.zeros((NB, MZ, LANES))
    own[:, :, :CY] = spread
    own[:, :, CY + 13 : CY + 16] = spread[:, :, 125:128]
    own[:, :, CY + 112 : CY + 115] = spread[:, :, 0:3]
    side = np.zeros((2, NB, MZ, CY))
    side[0, :, :, 96:112] = spread[:, :, 112:128]
    side[0, :, :, 125:128] = spread[:, :, 125:128]
    side[1, :, :, 16:32] = spread[:, :, 0:16]
    side[1, :, :, 0:3] = spread[:, :, 0:3]
    wave = np.broadcast_to(depth[1][:, None], (NZ, CY))
    mix = np.pad(mix, ((0, 0), (0, CY - MZ * CX)))
    parts = [own[:, s, k * CY : (k + 1) * CY] for s in range(MZ) for k in range(2)]
    parts += [side[:, :, s].reshape(2 * NB, CY) for s in range(MZ)]
    parts += [rows, mix, np.concatenate([near, near], axis=1), wave]
    return np.concatenate(parts, axis=0).astype(np.float32)


OWN, SIDE, MOMENT, MIX, NEAR, WAVE = 0, 256, 512, 576, 640, 648


def lane_shift(values, by):
    return pltpu.roll(values, by % values.shape[-1], axis=values.ndim - 1)


def depth_shift(values, by):
    return pltpu.roll(values, by % NZ, axis=0)


def lanes_in(shape, *ranges):
    lane = lax.broadcasted_iota(jnp.int32, shape, len(shape) - 1)
    inside = jnp.zeros(shape, jnp.bool_)
    for low, high in ranges:
        inside = inside | ((lane >= low) & (lane < high))
    return inside


def chebyshev():
    centre = (UPPER_BOUND + LOWER_BOUND) / 2.0
    radius = (UPPER_BOUND - LOWER_BOUND) / 2.0
    spread = centre / radius
    ratio = 1.0 / spread
    steps = []
    for _ in range(CHEB - 1):
        following = 1.0 / (2.0 * spread - ratio)
        steps.append((following * ratio, 2.0 * following / radius))
        ratio = following
    return 1.0 / centre, steps


def side_flux(values, south, below):
    across = south * (values - lane_shift(values, 1))
    upward = below * (values - depth_shift(values, 1))
    return (across - lane_shift(across, -1)) + (upward - depth_shift(upward, -1))


def spread_moments(r_row, table_ref, inv_ref, line_ref, out_ref):
    for x in range(CX):
        row = r_row(x)
        line_ref[x : x + 1, :] = jnp.sum(row, axis=0, keepdims=True)
        line_ref[CX + x : CX + x + 1, :] = jnp.sum(row * table_ref[WAVE : WAVE + NZ, :], axis=0, keepdims=True)
    mix = table_ref[MIX : MIX + NB, : MZ * CX]
    mixed = jnp.dot(mix, line_ref[...], precision=lax.Precision.HIGHEST, preferred_element_type=jnp.float32)
    moments = jnp.sum(mixed * table_ref[MOMENT : MOMENT + NB, :], axis=1, keepdims=True)
    column = jnp.broadcast_to(moments, (NB, CY))
    tiles = inv_ref.shape[1] // CY
    groups = tiles // 6
    out_ref[0, 0:1, :] = jnp.zeros((1, CY), jnp.float32)
    out_ref[groups - 1, WINDOW - 1 : WINDOW, :] = jnp.zeros((1, CY), jnp.float32)
    for t in range(tiles):
        total = jnp.sum(column * inv_ref[:, t * CY : (t + 1) * CY], axis=0, keepdims=True)
        for group in range(groups):
            place = t - (6 * group - 1)
            if 0 <= place < WINDOW:
                out_ref[group, place : place + 1, :] = total


def bit(place_ref, which):
    return ((place_ref[0] >> which) & 1) == 1


def own_kernel(place_ref, conc_hbm, label_hbm, out_ref, one_ref, two_ref, conc_ref, label_ref, sems):
    copies = [
        pltpu.make_async_copy(conc_hbm, conc_ref, sems.at[0]),
        pltpu.make_async_copy(label_hbm, label_ref, sems.at[1]),
    ]
    for copy in copies:
        copy.start()
    upper = bit(place_ref, 4)
    for kind, copy in enumerate(copies):
        copy.wait()
        for x in range(CX):
            out_ref[kind, x] = conc_ref[:, x, :] if kind == 0 else label_ref[:, x, :].astype(jnp.float32)
    for kind in range(2):
        for row in range(FAR):
            head, tail = out_ref[kind, row], out_ref[kind, CX - FAR + row]
            one_ref[kind, row] = jnp.where(upper, head, tail)
            two_ref[kind, row] = jnp.where(upper, tail, head)


def curve_rows(scale_ref, slope_ref, curve_ref):
    for n, ref in enumerate((scale_ref, slope_ref)):
        for k in range(8):
            curve_ref[8 * n + k : 8 * n + k + 1, :] = jnp.full((1, CY), ref[k], jnp.float32)


def pieces(place_ref, refs):
    near_one, near_two, far_one, far_two, own = refs
    odd, upper = bit(place_ref, 3), bit(place_ref, 4)

    def at(kind, row):
        if HALO <= row < HALO + CX:
            return own[kind, row - HALO]
        below = row < HALO
        if FAR <= row < HALO + 2 * CX:
            place = row - FAR if below else row - HALO - CX
            flag, one, two = odd, near_one, near_two
        else:
            place = row if below else row - HALO - 2 * CX
            flag, one, two = upper, far_one, far_two
        first, second = one[kind, place], two[kind, place]
        return jnp.where(flag, first, second) if below else jnp.where(flag, second, first)

    return at


def strip_kernel(place_ref, near_one, near_two, far_one, far_two, own, one_ref, two_ref):
    at = pieces(place_ref, (near_one, near_two, far_one, far_two, own))
    odd = bit(place_ref, 0)
    for pack in range(PACKS):
        up = jnp.zeros((NZ, CY), jnp.float32)
        down = jnp.zeros((NZ, CY), jnp.float32)
        for slot in range(8):
            index = pack * 8 + slot
            if index < 2 * ROWS:
                values = at(index // ROWS, index % ROWS)
                mask = lanes_in((NZ, CY), (slot * STRIP, (slot + 1) * STRIP))
                up = jnp.where(mask, lane_shift(values, slot * STRIP - (CY - STRIP)), up)
                down = jnp.where(mask, lane_shift(values, slot * STRIP), down)
        one_ref[pack] = jnp.where(odd, down, up)
        two_ref[pack] = jnp.where(odd, up, down)


class Beside:
    def __init__(self, first, second):
        self.first, self.second = first, second

    def __getitem__(self, row):
        return jnp.concatenate([self.first[row], self.second[row]], axis=1)


def each_row(step):
    def four(group, _):
        for k in range(4):
            step(4 * group + k)
        return 0

    lax.fori_loop(0, ROWS // 4, four, 0)
    for row in range(ROWS // 4 * 4, ROWS):
        step(row)


def diffusivity(conc, label, curve_ref):
    kind = label.astype(jnp.int32) & 7
    bits = [(kind & (1 << b)) != 0 for b in range(3)]

    def pick(table):
        layer = [jnp.broadcast_to(curve_ref[table + k : table + k + 1, :], conc.shape) for k in range(8)]
        for bit in bits:
            layer = [jnp.where(bit, layer[2 * n + 1], layer[2 * n]) for n in range(len(layer) // 2)]
        return layer[0]

    return pick(0) * jnp.exp(pick(8) * conc)


def pair_weight(a, b, la, lb):
    weight = jnp.where(la == lb, 0.5, 0.5 * CONTACT)
    return jnp.where(jnp.minimum(la, lb) > 0.5, weight * (a + b), 0.0)


def tile_faces(row, coeff, label, west, below):
    a, la = coeff[row], label[row]
    before = jnp.maximum(row - 1, 0)
    west[row] = pair_weight(a, coeff[before], la, label[before])
    not_bottom = lax.broadcasted_iota(jnp.int32, a.shape, 0) > 0
    below[row] = jnp.where(not_bottom, pair_weight(a, depth_shift(a, 1), la, depth_shift(la, 1)), 0.0)


def tile_sums(row, conc, west, below):
    following, before = jnp.minimum(row + 1, ROWS - 1), jnp.maximum(row - 1, 0)
    c, w, e, b = conc[row], west[row], west[following], below[row]
    upward = b * (c - depth_shift(c, 1))
    flux = e * (conc[following] - c) - w * (c - conc[before]) - (upward - depth_shift(upward, -1))
    return INVERSE_STEP + w + e + b + depth_shift(b, -1), flux


def tile_kernel(
    place_ref, scale_hbm, slope_hbm, inv_hbm, table_hbm, near_one, near_two, far_one, far_two, own,
    conc, label, coeff, west, below, diagonal, source, conc_edge, label_edge, curve_ref, inv_ref, table_ref,
    scale_ref, slope_ref, sems,
):
    sources = (scale_hbm, slope_hbm, inv_hbm, table_hbm)
    targets = (scale_ref, slope_ref, inv_ref, table_ref)
    copies = [pltpu.make_async_copy(a, b, sems.at[n]) for n, (a, b) in enumerate(zip(sources, targets))]
    for copy in copies:
        copy.start()
    at = pieces(place_ref, (near_one, near_two, far_one, far_two, own))
    end, start = lanes_in((NZ, CY), (13, 16)), lanes_in((NZ, CY), (112, 115))
    for kind, (target, edge) in enumerate(((conc, conc_edge), (label, label_edge))):
        for row in range(ROWS):
            values = at(kind, row)
            target[row] = values
            beside = jnp.where(end, lane_shift(values, 16), 0.0)
            edge[row] = jnp.where(start, lane_shift(values, -16), beside)
    copies[0].wait()
    copies[1].wait()
    curve_rows(scale_ref, slope_ref, curve_ref)

    def fill(row):
        coeff[row] = diffusivity(conc[row], label[row], curve_ref)

    each_row(fill)
    each_row(lambda row: tile_faces(row, coeff, label, west, below))

    def sums(row):
        diagonal[row], source[row] = tile_sums(row, conc, west, below)

    each_row(sums)
    copies[2].wait()
    copies[3].wait()


def setup_kernel(
    place_ref,
    conc0, label0, coeff0, west0, below0, diagonal0, source0, conc_edge, label_edge, curve_ref, inv_ref, table_ref,
    one_ref, two_ref,
    west1, below1, south_out, inverse_out, source_out, out_ref,
    conc1, label1, coeff1, line_ref,
):
    tile = (NZ, CY)
    m_right, m_right_own = lanes_in(tile, (16, 32)), lanes_in(tile, (0, 3))
    m_left, m_left_own = lanes_in(tile, (96, 112)), lanes_in(tile, (125, 128))
    odd = bit(place_ref, 0)
    for pack in range(PACKS):
        one, two = one_ref[pack], two_ref[pack]
        from_left, from_right = jnp.where(odd, one, two), jnp.where(odd, two, one)
        for part in range(8):
            index = pack * 8 + part
            if index >= 2 * ROWS:
                continue
            kind, row = index // ROWS, index % ROWS
            edge, second = ((conc_edge, conc1), (label_edge, label1))[kind]
            slot = part * STRIP
            merged = jnp.where(m_right, lane_shift(from_right, 16 - slot), edge[row])
            merged = jnp.where(m_right_own, lane_shift(from_right, -slot), merged)
            merged = jnp.where(m_left, lane_shift(from_left, 96 - slot), merged)
            second[row] = jnp.where(m_left_own, lane_shift(from_left, 112 - slot), merged)

    def fill(row):
        coeff1[row] = diffusivity(conc1[row], label1[row], curve_ref)

    each_row(fill)
    each_row(lambda row: tile_faces(row, coeff1, label1, west1, below1))
    coeff, label, conc = Beside(coeff0, coeff1), Beside(label0, label1), Beside(conc0, conc1)
    box = lanes_in((NZ, LANES), (0, 130), (142, 160), (224, 242), (254, 256))

    def operator(row):
        a, la, c = coeff[row], label[row], conc[row]
        south = pair_weight(a, lane_shift(a, 1), la, lane_shift(la, 1))
        south_out[row] = south
        diagonal1, source1 = tile_sums(row, conc1, west1, below1)
        diagonal = jnp.concatenate([diagonal0[row], diagonal1], axis=1) + south + lane_shift(south, -1)
        inverse_out[row] = jnp.where(box, 1.0 / diagonal, 0.0)
        across = south * (c - lane_shift(c, 1))
        source_out[row] = jnp.concatenate([source0[row], source1], axis=1) - (across - lane_shift(across, -1))

    each_row(operator)
    spread_moments(lambda x: source_out[HALO + x, :, :CY], table_ref, inv_ref, line_ref, out_ref)


def local_kernel(
    _, r_ref, west0, west1, south_ref, below0, below1, inverse_ref, out_ref, u_ref, q_ref, x_ref, *, wide
):
    west_ref, below_ref = Beside(west0, west1), Beside(below0, below1)
    scaled, steps = chebyshev()
    plus = lanes_in((NZ, LANES), (253, 256), (141, 144))
    minus = lanes_in((NZ, LANES), (128, 131), (240, 243))

    def solve(base, low, high, box_low, box_high, limit, u_ref, q_ref, x_ref):
        def start(row):
            if not box_low <= row <= box_high:
                return None
            return scaled * inverse_ref[base + row] * r_ref[base + row]

        def held(row):
            if not box_low <= row <= box_high:
                return None
            return u_ref[row - box_low]

        for number, (keep, gain) in enumerate(steps):
            more = len(steps) - 1 - number
            first, last = max(low - more, box_low), min(high + more, box_high)
            fetch = start if number == 0 else held
            now, before = fetch(first), fetch(first - 1)
            flow = west_ref[base + first] * (now if before is None else now - before)
            for row in range(first, last + 1):
                following = fetch(row + 1)
                if row + 1 < limit:
                    gate = west_ref[base + row + 1]
                    onward = gate * (-now if following is None else following - now)
                else:
                    onward = jnp.zeros_like(now)
                place = row - box_low
                applied = INVERSE_STEP * now + (flow - onward)
                applied = applied + side_flux(now, south_ref[base + row], below_ref[base + row])
                remain = (r_ref[base + row] if number == 0 else q_ref[place]) - applied
                step = keep * now + gain * (inverse_ref[base + row] * remain)
                if more:
                    u_ref[place] = step
                    q_ref[place] = remain
                if low <= row <= high:
                    result = (now if number == 0 else x_ref[place]) + step
                    if more:
                        x_ref[place] = result
                    else:
                        merged = jnp.where(plus, lane_shift(result, 16), result)
                        out_ref[base + row] = jnp.where(minus, lane_shift(result, -16), merged)
                now, flow = following, onward

    whole = [-1, 0, 1] if wide >= 5 else []
    for block in range(-2, 3):
        low, high = max(-wide, 8 * block), min(CX - 1 + wide, 8 * block + 7)
        if low > high or block in whole:
            continue
        base = HALO + 8 * block
        box_low, box_high = max(8 * block - OV, -HALO), min(8 * block + 7 + OV, CX - 1 + HALO)
        at = lambda row: row - 8 * block
        boxes = (ref.at[block % 3] for ref in (u_ref, q_ref, x_ref))
        solve(base, at(low), at(high), at(box_low), at(box_high), ROWS - base, *boxes)
    if whole:

        def body(number, _):
            boxes = (ref.at[0] for ref in (u_ref, q_ref, x_ref))
            solve(HALO + 8 * (number + whole[0]), 0, CX - 1, -OV, CX - 1 + OV, CX + OV + 1, *boxes)
            return 0

        lax.fori_loop(0, len(whole), body, 0)


def turn_kernel(in_ref, out_ref):
    total = in_ref[0]
    for peer in range(1, in_ref.shape[0]):
        total = total + in_ref[peer]
    for z in range(N_Z):
        out_ref[z] = total[z // 2 : z // 2 + SPAN, :]


def answer_kernel(in_ref, out_ref):
    total = in_ref[0]
    for peer in range(1, N_Z):
        total = total + in_ref[peer]
    out_ref[...] = total


def coarse_rows(odd, answers, table_ref, flat_ref, wavy_ref):
    near = table_ref[NEAR : NEAR + CX, :]
    left_half = lanes_in((SPAN, CY), (0, NB))

    def blocks(low, high):
        turned = [lane_shift(a, NB) for a in (low, high)]
        even, uneven = jnp.where(left_half, low, turned[1]), jnp.where(left_half, turned[0], high)
        rows = []
        for block in range(5):
            choice = []
            for index in (block, block + 1):
                source = uneven if index % 2 else even
                choice.append(jnp.broadcast_to(source[index // 2 : index // 2 + 1, :], (CX, CY)))
            rows.append(jnp.where(odd, choice[1], choice[0]) * near)
        return jnp.concatenate(rows, axis=0)

    left, own, right = answers
    own, sides = blocks(own, own)[:, :NB], blocks(left, right)
    dot = functools.partial(jnp.dot, precision=lax.Precision.HIGHEST, preferred_element_type=jnp.float32)
    own_at = lambda n: dot(own, table_ref[OWN + n * NB : OWN + (n + 1) * NB, :])
    for s, target in enumerate((flat_ref, wavy_ref)):
        first = SIDE + s * 2 * NB
        target[:, :CY] = own_at(2 * s)
        target[:, CY:] = own_at(2 * s + 1) + dot(sides, table_ref[first : first + 2 * NB, :])


def update_kernel(*refs, reach, first):
    refs = list(refs)
    take = lambda count: [refs.pop(0) for _ in range(count)]
    place_ref, one_ref, own_ref, two_ref = take(4)
    right_column = bit(place_ref, 0)
    one, two = one_ref[...], two_ref[...]
    answers = (jnp.where(right_column, one, two), own_ref[...], jnp.where(right_column, two, one))
    x_ref, source_ref, west0, west1, south_ref, below0, below1 = take(7)
    west_ref, below_ref = Beside(west0, west1), Beside(below0, below1)
    (table_ref,) = take(1)
    (old_ref,) = take(0 if first else 1) or (None,)
    if reach:
        (inv_ref,) = take(1)
        u_ref, r_ref, out_ref = take(3)
        flat_ref, wavy_ref, line_ref = take(3)
    else:
        (packed_ref,) = take(1)
        updated_ref, residual_ref = take(2)
        flat_ref, wavy_ref = take(2)
        u_ref = None
    coarse_rows(bit(place_ref, 3), answers, table_ref, flat_ref, wavy_ref)
    wave = table_ref[WAVE : WAVE + NZ, :]
    wave = jnp.concatenate([wave, wave], axis=1)

    def fresh(row):
        place = row + 2 * CX
        field = jnp.broadcast_to(flat_ref[place : place + 1, :], (NZ, LANES))
        field = field + wave * jnp.broadcast_to(wavy_ref[place : place + 1, :], (NZ, LANES))
        value = x_ref[row + HALO] + field
        if not first:
            value = old_ref[row + HALO] + value
        if u_ref is not None:
            u_ref[row + HALO] = value
        return value

    if reach:
        for row in (-reach - 2, -reach - 1, CX + reach, CX + reach + 1):
            r_ref[row + HALO] = jnp.zeros((NZ, LANES), jnp.float32)
    before, now = fresh(-reach - 1), fresh(-reach)
    flow = west_ref[HALO - reach] * (now - before)
    for row in range(-reach, CX + reach):
        following = fresh(row + 1)
        onward = west_ref[row + 1 + HALO] * (following - now)
        applied = INVERSE_STEP * now + (flow - onward)
        applied = applied + side_flux(now, south_ref[row + HALO], below_ref[row + HALO])
        remain = source_ref[row + HALO] - applied
        if reach:
            r_ref[row + HALO] = remain
        else:
            updated_ref[:, row, :] = packed_ref[0, row] + now[:, :CY]
            residual_ref[:, row, :] = remain[:, :CY]
        now, flow = following, onward
    if reach:
        spread_moments(lambda x: r_ref[HALO + x, :, :CY], table_ref, inv_ref, line_ref, out_ref)


def vmem(count):
    return [pl.BlockSpec(memory_space=pltpu.VMEM)] * count


def shaped(*shape):
    return jax.ShapeDtypeStruct(shape, jnp.float32)


def swapped(array, axis, apart):
    size = lax.axis_size(axis)
    arrays = array if isinstance(array, (list, tuple)) else (array, array)
    results = []
    for offset, values in zip((0, apart), arrays):
        pairs = []
        for low in range(size - apart):
            if (low - offset) % (2 * apart) < apart:
                pairs += [(low, low + apart), (low + apart, low)]
        results.append(lax.ppermute(values, axis, pairs))
    return results


def room(mebibytes):
    return pltpu.CompilerParams(vmem_limit_bytes=mebibytes * 2**20)


def cost(flops, accessed=4_000_000):
    return pl.CostEstimate(flops=flops, bytes_accessed=accessed, transcendentals=0)


def on_device(concentration, labels, curve_scale, curve_slope, coarse_inv):
    size = lax.axis_size("gx")
    n_y = size // N_Z
    along_z = [[y * N_Z + z for z in range(N_Z)] for y in range(n_y)]
    along_y = [[y * N_Z + z for y in range(n_y)] for z in range(N_Z)]
    place = (8 * lax.axis_index("gx") + lax.axis_index("gy")).astype(jnp.int32).reshape(1)
    place, concentration = lax.optimization_barrier((place, concentration))
    frame = shaped(ROWS, NZ, LANES)
    smem, anywhere = pl.BlockSpec(memory_space=pltpu.SMEM), pl.BlockSpec(memory_space=pl.ANY)
    scratch = lambda *shape: pltpu.VMEM(shape, jnp.float32)
    line_scratch = scratch(MZ * CX, CY)
    table_scratch = [scratch(5 * CX, LANES)] * 2

    kept = lambda array: pltpu.with_memory_space_constraint(array, pltpu.HBM)
    hbm = pl.BlockSpec(memory_space=pltpu.HBM)
    own, *far = pl.pallas_call(
        own_kernel,
        out_shape=[shaped(2, CX, NZ, CY)] + [shaped(2, FAR, NZ, CY)] * 2,
        in_specs=[smem, hbm, hbm],
        out_specs=vmem(3),
        scratch_shapes=[scratch(NZ, CX, CY), pltpu.VMEM((NZ, CX, CY), jnp.int32), pltpu.SemaphoreType.DMA((2,))],
        compiler_params=room(4),
        name="own",
    )(place, kept(concentration), kept(labels))
    parts = (*swapped(own, "gx", 1), *swapped(far, "gx", 2), own)
    strips = pl.pallas_call(
        strip_kernel,
        out_shape=[shaped(PACKS, NZ, CY)] * 2,
        in_specs=[smem] + vmem(5),
        out_specs=vmem(2),
        compiler_params=room(4),
        name="strips",
    )(place, *parts)
    strips = swapped(strips, "gy", 1)
    half_frame = shaped(ROWS, NZ, CY)
    table = tables()
    tiled = pl.pallas_call(
        tile_kernel,
        out_shape=[half_frame] * 9 + [shaped(16, CY), shaped(NB, NB * size), shaped(*table.shape)],
        in_specs=[smem] + [hbm] * 4 + vmem(5),
        out_specs=vmem(12),
        scratch_shapes=[pltpu.SMEM((8,), jnp.float32)] * 2 + [pltpu.SemaphoreType.DMA((4,))],
        compiler_params=room(4),
        cost_estimate=cost(10_000_000),
        name="tile",
    )(place, *(kept(a) for a in (curve_scale, curve_slope, coarse_inv[0], jnp.asarray(table))), *parts)
    west0, below0 = tiled[3:5]
    inverse_rows, table = tiled[10:]
    west1, below1, south, inverse, source, partial = pl.pallas_call(
        setup_kernel,
        out_shape=[half_frame] * 2 + [frame] * 3 + [shaped(n_y, WINDOW, CY)],
        in_specs=[smem] + vmem(14),
        out_specs=vmem(6),
        scratch_shapes=[scratch(ROWS, NZ, CY)] * 3 + [line_scratch],
        compiler_params=room(8),
        name="setup",
    )(place, *tiled, *strips)
    faces = (west0, west1, south, below0, below1)

    residual, update = source, None
    for sweep, reach in enumerate(REACH):
        through = lax.all_to_all(partial, "gx", 0, 0, tiled=True, axis_index_groups=along_y)
        turned = pl.pallas_call(
            turn_kernel,
            out_shape=shaped(N_Z, SPAN, CY),
            in_specs=vmem(1),
            out_specs=vmem(1)[0],
            compiler_params=room(4),
            name="turn",
        )(through)
        arrived = lax.all_to_all(turned, "gx", 0, 0, tiled=True, axis_index_groups=along_z)
        answer = pl.pallas_call(
            answer_kernel,
            out_shape=shaped(SPAN, CY),
            in_specs=vmem(1),
            out_specs=vmem(1)[0],
            compiler_params=room(4),
            name="answer",
        )(arrived)
        one, two = swapped(answer, "gy", 1)
        local = pl.pallas_call(
            functools.partial(local_kernel, wide=reach + 1),
            out_shape=frame,
            in_specs=[anywhere] + vmem(7),
            out_specs=vmem(1)[0],
            scratch_shapes=[scratch(3, CX + 2 * OV, NZ, LANES)] * 3,
            compiler_params=room(8),
            cost_estimate=cost(20_000_000),
            name="local",
        )(answer, residual, *faces, inverse)
        operands = [place, one, answer, two, local, source, *faces, table]
        operands += [] if sweep == 0 else [update]
        kernel = functools.partial(update_kernel, reach=reach, first=sweep == 0)
        if reach:
            operands += [inverse_rows]
            update, residual, partial = pl.pallas_call(
                kernel,
                out_shape=[frame, frame, shaped(n_y, WINDOW, CY)],
                in_specs=[smem] + vmem(len(operands) - 1),
                out_specs=vmem(3),
                scratch_shapes=table_scratch + [line_scratch],
                compiler_params=room(8),
                name="update",
            )(*operands)
        else:
            operands += [own]
            return pl.pallas_call(
                kernel,
                out_shape=[shaped(NZ, CX, CY)] * 2,
                in_specs=[smem] + vmem(len(operands) - 1),
                out_specs=vmem(2),
                scratch_shapes=table_scratch,
                compiler_params=room(8),
                name="final",
            )(*operands)


def solution(mesh):
    return jax.shard_map(
        on_device,
        mesh=mesh,
        in_specs=(P(None, "gx", "gy"), P(None, "gx", "gy"), P(), P(), P("gy", "gx", None)),
        out_specs=(P(None, "gx", "gy"), P(None, "gx", "gy")),
        check_vma=False,
    )
```

```python
import functools
import math

import jax
import jax.numpy as jnp
import numpy as np
from jax import lax
from jax.experimental import pallas as pl
from jax.experimental.pallas import tpu as pltpu
from jax.sharding import PartitionSpec as P

NZ = 16
CX = 8
CY = 128
OV = 2
SWEEPS = 3
CHEB = 4
MZ = 2
MX = 4
MY = 8
NB = 64
N_Z = 12
INVERSE_STEP = 0.004
CONTACT = 0.3
LOWER_BOUND = 0.1
UPPER_BOUND = 1.9

HALO = 13
ROWS = CX + 2 * HALO
FAR = HALO - CX
LANES = 256
STRIP = 16
WINDOW = 8
SPAN = 3
REACH = (8, 4, 0)
PACKS = 9


def cosine_table(mode_count, length):
    position = np.arange(length) + 0.5
    order = np.arange(mode_count)
    scaling = np.where(order == 0, math.sqrt(1.0 / length), math.sqrt(2.0 / length))
    return scaling[:, None] * np.cos(math.pi * order[:, None] * position[None, :] / length)


def tables():
    depth, first, second = cosine_table(MZ, NZ), cosine_table(MX, CX), cosine_table(MY, CY)
    flat = depth[0, 0]
    mix = np.zeros((NB, MZ * CX))
    rows = np.zeros((NB, CY))
    for s in range(MZ):
        for p in range(MX):
            for q in range(MY):
                n = (s * MX + p) * MY + q
                mix[n, s * CX : (s + 1) * CX] = first[p] * (flat if s == 0 else 1.0)
                rows[n] = second[q]
    near = np.zeros((CX, NB))
    spread = np.zeros((NB, MZ, CY))
    for s in range(MZ):
        for p in range(MX):
            for q in range(MY):
                n = (s * MX + p) * MY + q
                near[:, n] = first[p]
                spread[n, s] = second[q] * (flat if s == 0 else 1.0)
    own = np.zeros((NB, MZ, LANES))
    own[:, :, :CY] = spread
    own[:, :, CY + 13 : CY + 16] = spread[:, :, 125:128]
    own[:, :, CY + 112 : CY + 115] = spread[:, :, 0:3]
    side = np.zeros((2, NB, MZ, CY))
    side[0, :, :, 96:112] = spread[:, :, 112:128]
    side[0, :, :, 125:128] = spread[:, :, 125:128]
    side[1, :, :, 16:32] = spread[:, :, 0:16]
    side[1, :, :, 0:3] = spread[:, :, 0:3]
    wave = np.broadcast_to(np.concatenate([depth[1][0::2], depth[1][1::2]])[:, None], (NZ, CY))
    mix = np.pad(mix, ((0, 0), (0, CY - MZ * CX)))
    parts = [own[:, s, k * CY : (k + 1) * CY] for s in range(MZ) for k in range(2)]
    parts += [side[:, :, s].reshape(2 * NB, CY) for s in range(MZ)]
    parts += [rows, mix, np.concatenate([near, near], axis=1), wave]
    return np.concatenate(parts, axis=0).astype(np.float32)


OWN, SIDE, MOMENT, MIX, NEAR, WAVE = 0, 256, 512, 576, 640, 648


def lane_shift(values, by):
    return pltpu.roll(values, by % values.shape[-1], axis=values.ndim - 1)


def depth_shift(values, by):
    even, uneven = values[: NZ // 2], values[NZ // 2 :]
    if by > 0:
        return jnp.concatenate([pltpu.roll(uneven, 1, axis=0), even], axis=0)
    return jnp.concatenate([uneven, pltpu.roll(even, NZ // 2 - 1, axis=0)], axis=0)


def depths(parity):
    return pl.ds(parity, NZ // 2, stride=2)


def lanes_in(shape, *ranges):
    lane = lax.broadcasted_iota(jnp.int32, shape, len(shape) - 1)
    inside = jnp.zeros(shape, jnp.bool_)
    for low, high in ranges:
        inside = inside | ((lane >= low) & (lane < high))
    return inside


def chebyshev():
    centre = (UPPER_BOUND + LOWER_BOUND) / 2.0
    radius = (UPPER_BOUND - LOWER_BOUND) / 2.0
    spread = centre / radius
    ratio = 1.0 / spread
    steps = []
    for _ in range(CHEB - 1):
        following = 1.0 / (2.0 * spread - ratio)
        steps.append((following * ratio, 2.0 * following / radius))
        ratio = following
    return 1.0 / centre, steps


def side_flux(values, south, below):
    across = south * (values - lane_shift(values, 1))
    upward = below * (values - depth_shift(values, 1))
    return (across - lane_shift(across, -1)) + (upward - depth_shift(upward, -1))


def spread_moments(r_row, table_ref, inv_ref, line_ref, out_ref):
    for x in range(CX):
        row = r_row(x)
        line_ref[x : x + 1, :] = jnp.sum(row, axis=0, keepdims=True)
        line_ref[CX + x : CX + x + 1, :] = jnp.sum(row * table_ref[WAVE : WAVE + NZ, :], axis=0, keepdims=True)
    mix = table_ref[MIX : MIX + NB, : MZ * CX]
    mixed = jnp.dot(mix, line_ref[...], precision=lax.Precision.HIGHEST, preferred_element_type=jnp.float32)
    moments = jnp.sum(mixed * table_ref[MOMENT : MOMENT + NB, :], axis=1, keepdims=True)
    column = jnp.broadcast_to(moments, (NB, CY))
    tiles = inv_ref.shape[1] // CY
    groups = tiles // 6
    out_ref[0, 0:1, :] = jnp.zeros((1, CY), jnp.float32)
    out_ref[groups - 1, WINDOW - 1 : WINDOW, :] = jnp.zeros((1, CY), jnp.float32)
    for t in range(tiles):
        total = jnp.sum(column * inv_ref[:, t * CY : (t + 1) * CY], axis=0, keepdims=True)
        for group in range(groups):
            place = t - (6 * group - 1)
            if 0 <= place < WINDOW:
                out_ref[group, place : place + 1, :] = total


def bit(place_ref, which):
    return ((place_ref[0] >> which) & 1) == 1


def own_kernel(place_ref, conc_hbm, label_hbm, out_ref, one_ref, two_ref, conc_ref, label_ref, sems):
    copies = [
        pltpu.make_async_copy(conc_hbm, conc_ref, sems.at[0]),
        pltpu.make_async_copy(label_hbm, label_ref, sems.at[1]),
    ]
    for copy in copies:
        copy.start()
    upper = bit(place_ref, 4)
    for kind, copy in enumerate(copies):
        copy.wait()
        for x in range(CX):
            for parity in range(2):
                values = (conc_ref, label_ref)[kind][depths(parity), x, :]
                out_ref[kind, x, parity * NZ // 2 : (parity + 1) * NZ // 2] = values.astype(jnp.float32)
    for kind in range(2):
        for row in range(FAR):
            head, tail = out_ref[kind, row], out_ref[kind, CX - FAR + row]
            one_ref[kind, row] = jnp.where(upper, head, tail)
            two_ref[kind, row] = jnp.where(upper, tail, head)


def curve_rows(scale_ref, slope_ref, curve_ref):
    for n, ref in enumerate((scale_ref, slope_ref)):
        for k in range(8):
            curve_ref[8 * n + k : 8 * n + k + 1, :] = jnp.full((1, CY), ref[k], jnp.float32)


def pieces(place_ref, refs):
    near_one, near_two, far_one, far_two, own = refs
    odd, upper = bit(place_ref, 3), bit(place_ref, 4)

    def at(kind, row):
        if HALO <= row < HALO + CX:
            return own[kind, row - HALO]
        below = row < HALO
        if FAR <= row < HALO + 2 * CX:
            place = row - FAR if below else row - HALO - CX
            flag, one, two = odd, near_one, near_two
        else:
            place = row if below else row - HALO - 2 * CX
            flag, one, two = upper, far_one, far_two
        first, second = one[kind, place], two[kind, place]
        return jnp.where(flag, first, second) if below else jnp.where(flag, second, first)

    return at


def strip_kernel(place_ref, near_one, near_two, far_one, far_two, own, one_ref, two_ref):
    at = pieces(place_ref, (near_one, near_two, far_one, far_two, own))
    odd = bit(place_ref, 0)
    for pack in range(PACKS):
        up = jnp.zeros((NZ, CY), jnp.float32)
        down = jnp.zeros((NZ, CY), jnp.float32)
        for slot in range(8):
            index = pack * 8 + slot
            if index < 2 * ROWS:
                values = at(index // ROWS, index % ROWS)
                mask = lanes_in((NZ, CY), (slot * STRIP, (slot + 1) * STRIP))
                up = jnp.where(mask, lane_shift(values, slot * STRIP - (CY - STRIP)), up)
                down = jnp.where(mask, lane_shift(values, slot * STRIP), down)
        one_ref[pack] = jnp.where(odd, down, up)
        two_ref[pack] = jnp.where(odd, up, down)


class Beside:
    def __init__(self, first, second):
        self.first, self.second = first, second

    def __getitem__(self, row):
        return jnp.concatenate([self.first[row], self.second[row]], axis=1)


def each_row(step):
    def four(group, _):
        for k in range(4):
            step(4 * group + k)
        return 0

    lax.fori_loop(0, ROWS // 4, four, 0)
    for row in range(ROWS // 4 * 4, ROWS):
        step(row)


def diffusivity(conc, label, curve_ref):
    kind = label.astype(jnp.int32) & 7
    bits = [(kind & (1 << b)) != 0 for b in range(3)]

    def pick(table):
        layer = [jnp.broadcast_to(curve_ref[table + k : table + k + 1, :], conc.shape) for k in range(8)]
        for bit in bits:
            layer = [jnp.where(bit, layer[2 * n + 1], layer[2 * n]) for n in range(len(layer) // 2)]
        return layer[0]

    return pick(0) * jnp.exp(pick(8) * conc)


def pair_weight(a, b, la, lb):
    weight = jnp.where(la == lb, 0.5, 0.5 * CONTACT)
    return jnp.where(jnp.minimum(la, lb) > 0.5, weight * (a + b), 0.0)


def tile_faces(row, coeff, label, west, below):
    a, la = coeff[row], label[row]
    before = jnp.maximum(row - 1, 0)
    west[row] = pair_weight(a, coeff[before], la, label[before])
    not_bottom = lax.broadcasted_iota(jnp.int32, a.shape, 0) > 0
    below[row] = jnp.where(not_bottom, pair_weight(a, depth_shift(a, 1), la, depth_shift(la, 1)), 0.0)


def tile_sums(row, conc, west, below):
    following, before = jnp.minimum(row + 1, ROWS - 1), jnp.maximum(row - 1, 0)
    c, w, e, b = conc[row], west[row], west[following], below[row]
    upward = b * (c - depth_shift(c, 1))
    flux = e * (conc[following] - c) - w * (c - conc[before]) - (upward - depth_shift(upward, -1))
    return INVERSE_STEP + w + e + b + depth_shift(b, -1), flux


def tile_kernel(
    place_ref, scale_hbm, slope_hbm, inv_hbm, table_hbm, near_one, near_two, far_one, far_two, own,
    conc, label, coeff, west, below, diagonal, source, conc_edge, label_edge, curve_ref, inv_ref, table_ref,
    scale_ref, slope_ref, sems,
):
    sources = (scale_hbm, slope_hbm, inv_hbm, table_hbm)
    targets = (scale_ref, slope_ref, inv_ref, table_ref)
    copies = [pltpu.make_async_copy(a, b, sems.at[n]) for n, (a, b) in enumerate(zip(sources, targets))]
    for copy in copies:
        copy.start()
    at = pieces(place_ref, (near_one, near_two, far_one, far_two, own))
    end, start = lanes_in((NZ, CY), (13, 16)), lanes_in((NZ, CY), (112, 115))
    for kind, (target, edge) in enumerate(((conc, conc_edge), (label, label_edge))):
        for row in range(ROWS):
            values = at(kind, row)
            target[row] = values
            beside = jnp.where(end, lane_shift(values, 16), 0.0)
            edge[row] = jnp.where(start, lane_shift(values, -16), beside)
    copies[0].wait()
    copies[1].wait()
    curve_rows(scale_ref, slope_ref, curve_ref)

    def fill(row):
        coeff[row] = diffusivity(conc[row], label[row], curve_ref)

    each_row(fill)
    each_row(lambda row: tile_faces(row, coeff, label, west, below))

    def sums(row):
        diagonal[row], source[row] = tile_sums(row, conc, west, below)

    each_row(sums)
    copies[2].wait()
    copies[3].wait()


def setup_kernel(
    place_ref,
    conc0, label0, coeff0, west0, below0, diagonal0, source0, conc_edge, label_edge, curve_ref, inv_ref, table_ref,
    one_ref, two_ref,
    west1, below1, south_out, inverse_out, source_out, out_ref,
    conc1, label1, coeff1, line_ref,
):
    tile = (NZ, CY)
    m_right, m_right_own = lanes_in(tile, (16, 32)), lanes_in(tile, (0, 3))
    m_left, m_left_own = lanes_in(tile, (96, 112)), lanes_in(tile, (125, 128))
    odd = bit(place_ref, 0)
    for pack in range(PACKS):
        one, two = one_ref[pack], two_ref[pack]
        from_left, from_right = jnp.where(odd, one, two), jnp.where(odd, two, one)
        for part in range(8):
            index = pack * 8 + part
            if index >= 2 * ROWS:
                continue
            kind, row = index // ROWS, index % ROWS
            edge, second = ((conc_edge, conc1), (label_edge, label1))[kind]
            slot = part * STRIP
            merged = jnp.where(m_right, lane_shift(from_right, 16 - slot), edge[row])
            merged = jnp.where(m_right_own, lane_shift(from_right, -slot), merged)
            merged = jnp.where(m_left, lane_shift(from_left, 96 - slot), merged)
            second[row] = jnp.where(m_left_own, lane_shift(from_left, 112 - slot), merged)

    def fill(row):
        coeff1[row] = diffusivity(conc1[row], label1[row], curve_ref)

    each_row(fill)
    each_row(lambda row: tile_faces(row, coeff1, label1, west1, below1))
    coeff, label, conc = Beside(coeff0, coeff1), Beside(label0, label1), Beside(conc0, conc1)
    box = lanes_in((NZ, LANES), (0, 130), (142, 160), (224, 242), (254, 256))

    def operator(row):
        a, la, c = coeff[row], label[row], conc[row]
        south = pair_weight(a, lane_shift(a, 1), la, lane_shift(la, 1))
        south_out[row] = south
        diagonal1, source1 = tile_sums(row, conc1, west1, below1)
        diagonal = jnp.concatenate([diagonal0[row], diagonal1], axis=1) + south + lane_shift(south, -1)
        inverse_out[row] = jnp.where(box, 1.0 / diagonal, 0.0)
        across = south * (c - lane_shift(c, 1))
        source_out[row] = jnp.concatenate([source0[row], source1], axis=1) - (across - lane_shift(across, -1))

    each_row(operator)
    spread_moments(lambda x: source_out[HALO + x, :, :CY], table_ref, inv_ref, line_ref, out_ref)


def local_kernel(
    _, r_ref, west0, west1, south_ref, below0, below1, inverse_ref, out_ref, u_ref, q_ref, x_ref, *, wide
):
    west_ref, below_ref = Beside(west0, west1), Beside(below0, below1)
    scaled, steps = chebyshev()
    plus = lanes_in((NZ, LANES), (253, 256), (141, 144))
    minus = lanes_in((NZ, LANES), (128, 131), (240, 243))

    def solve(base, low, high, box_low, box_high, limit, u_ref, q_ref, x_ref):
        def start(row):
            if not box_low <= row <= box_high:
                return None
            return scaled * inverse_ref[base + row] * r_ref[base + row]

        def held(row):
            if not box_low <= row <= box_high:
                return None
            return u_ref[row - box_low]

        for number, (keep, gain) in enumerate(steps):
            more = len(steps) - 1 - number
            first, last = max(low - more, box_low), min(high + more, box_high)
            fetch = start if number == 0 else held
            now, before = fetch(first), fetch(first - 1)
            flow = west_ref[base + first] * (now if before is None else now - before)
            for row in range(first, last + 1):
                following = fetch(row + 1)
                if row + 1 < limit:
                    gate = west_ref[base + row + 1]
                    onward = gate * (-now if following is None else following - now)
                else:
                    onward = jnp.zeros_like(now)
                place = row - box_low
                applied = INVERSE_STEP * now + (flow - onward)
                applied = applied + side_flux(now, south_ref[base + row], below_ref[base + row])
                remain = (r_ref[base + row] if number == 0 else q_ref[place]) - applied
                step = keep * now + gain * (inverse_ref[base + row] * remain)
                if more:
                    u_ref[place] = step
                    q_ref[place] = remain
                if low <= row <= high:
                    result = (now if number == 0 else x_ref[place]) + step
                    if more:
                        x_ref[place] = result
                    else:
                        merged = jnp.where(plus, lane_shift(result, 16), result)
                        out_ref[base + row] = jnp.where(minus, lane_shift(result, -16), merged)
                now, flow = following, onward

    whole = [-1, 0, 1] if wide >= 5 else []
    for block in range(-2, 3):
        low, high = max(-wide, 8 * block), min(CX - 1 + wide, 8 * block + 7)
        if low > high or block in whole:
            continue
        base = HALO + 8 * block
        box_low, box_high = max(8 * block - OV, -HALO), min(8 * block + 7 + OV, CX - 1 + HALO)
        at = lambda row: row - 8 * block
        boxes = (ref.at[block % 3] for ref in (u_ref, q_ref, x_ref))
        solve(base, at(low), at(high), at(box_low), at(box_high), ROWS - base, *boxes)
    if whole:

        def body(number, _):
            boxes = (ref.at[0] for ref in (u_ref, q_ref, x_ref))
            solve(HALO + 8 * (number + whole[0]), 0, CX - 1, -OV, CX - 1 + OV, CX + OV + 1, *boxes)
            return 0

        lax.fori_loop(0, len(whole), body, 0)


def turn_kernel(in_ref, out_ref):
    total = in_ref[0]
    for peer in range(1, in_ref.shape[0]):
        total = total + in_ref[peer]
    for z in range(N_Z):
        out_ref[z] = total[z // 2 : z // 2 + SPAN, :]


def answer_kernel(in_ref, out_ref):
    total = in_ref[0]
    for peer in range(1, N_Z):
        total = total + in_ref[peer]
    out_ref[...] = total


def coarse_rows(odd, answers, table_ref, flat_ref, wavy_ref):
    near = table_ref[NEAR : NEAR + CX, :]
    left_half = lanes_in((SPAN, CY), (0, NB))

    def blocks(low, high):
        turned = [lane_shift(a, NB) for a in (low, high)]
        even, uneven = jnp.where(left_half, low, turned[1]), jnp.where(left_half, turned[0], high)
        rows = []
        for block in range(5):
            choice = []
            for index in (block, block + 1):
                source = uneven if index % 2 else even
                choice.append(jnp.broadcast_to(source[index // 2 : index // 2 + 1, :], (CX, CY)))
            rows.append(jnp.where(odd, choice[1], choice[0]) * near)
        return jnp.concatenate(rows, axis=0)

    left, own, right = answers
    own, sides = blocks(own, own)[:, :NB], blocks(left, right)
    dot = functools.partial(jnp.dot, precision=lax.Precision.HIGHEST, preferred_element_type=jnp.float32)
    own_at = lambda n: dot(own, table_ref[OWN + n * NB : OWN + (n + 1) * NB, :])
    for s, target in enumerate((flat_ref, wavy_ref)):
        first = SIDE + s * 2 * NB
        target[:, :CY] = own_at(2 * s)
        target[:, CY:] = own_at(2 * s + 1) + dot(sides, table_ref[first : first + 2 * NB, :])


def update_kernel(*refs, reach, first):
    refs = list(refs)
    take = lambda count: [refs.pop(0) for _ in range(count)]
    place_ref, one_ref, own_ref, two_ref = take(4)
    right_column = bit(place_ref, 0)
    one, two = one_ref[...], two_ref[...]
    answers = (jnp.where(right_column, one, two), own_ref[...], jnp.where(right_column, two, one))
    x_ref, source_ref, west0, west1, south_ref, below0, below1 = take(7)
    west_ref, below_ref = Beside(west0, west1), Beside(below0, below1)
    (table_ref,) = take(1)
    (old_ref,) = take(0 if first else 1) or (None,)
    if reach:
        (inv_ref,) = take(1)
        u_ref, r_ref, out_ref = take(3)
        flat_ref, wavy_ref, line_ref = take(3)
    else:
        (packed_ref,) = take(1)
        updated_ref, residual_ref = take(2)
        flat_ref, wavy_ref = take(2)
        u_ref = None
    coarse_rows(bit(place_ref, 3), answers, table_ref, flat_ref, wavy_ref)
    wave = table_ref[WAVE : WAVE + NZ, :]
    wave = jnp.concatenate([wave, wave], axis=1)

    def fresh(row):
        place = row + 2 * CX
        field = jnp.broadcast_to(flat_ref[place : place + 1, :], (NZ, LANES))
        field = field + wave * jnp.broadcast_to(wavy_ref[place : place + 1, :], (NZ, LANES))
        value = x_ref[row + HALO] + field
        if not first:
            value = old_ref[row + HALO] + value
        if u_ref is not None:
            u_ref[row + HALO] = value
        return value

    if reach:
        for row in (-reach - 2, -reach - 1, CX + reach, CX + reach + 1):
            r_ref[row + HALO] = jnp.zeros((NZ, LANES), jnp.float32)
    before, now = fresh(-reach - 1), fresh(-reach)
    flow = west_ref[HALO - reach] * (now - before)
    for row in range(-reach, CX + reach):
        following = fresh(row + 1)
        onward = west_ref[row + 1 + HALO] * (following - now)
        applied = INVERSE_STEP * now + (flow - onward)
        applied = applied + side_flux(now, south_ref[row + HALO], below_ref[row + HALO])
        remain = source_ref[row + HALO] - applied
        if reach:
            r_ref[row + HALO] = remain
        else:
            for target, values in ((updated_ref, packed_ref[0, row] + now[:, :CY]), (residual_ref, remain[:, :CY])):
                target[depths(0), row, :] = values[: NZ // 2]
                target[depths(1), row, :] = values[NZ // 2 :]
        now, flow = following, onward
    if reach:
        spread_moments(lambda x: r_ref[HALO + x, :, :CY], table_ref, inv_ref, line_ref, out_ref)


def vmem(count):
    return [pl.BlockSpec(memory_space=pltpu.VMEM)] * count


def shaped(*shape):
    return jax.ShapeDtypeStruct(shape, jnp.float32)


def swapped(array, axis, apart):
    size = lax.axis_size(axis)
    arrays = array if isinstance(array, (list, tuple)) else (array, array)
    results = []
    for offset, values in zip((0, apart), arrays):
        pairs = []
        for low in range(size - apart):
            if (low - offset) % (2 * apart) < apart:
                pairs += [(low, low + apart), (low + apart, low)]
        results.append(lax.ppermute(values, axis, pairs))
    return results


def room(mebibytes):
    return pltpu.CompilerParams(vmem_limit_bytes=mebibytes * 2**20)


def cost(flops, accessed=4_000_000):
    return pl.CostEstimate(flops=flops, bytes_accessed=accessed, transcendentals=0)


def on_device(concentration, labels, curve_scale, curve_slope, coarse_inv):
    size = lax.axis_size("gx")
    n_y = size // N_Z
    along_z = [[y * N_Z + z for z in range(N_Z)] for y in range(n_y)]
    along_y = [[y * N_Z + z for y in range(n_y)] for z in range(N_Z)]
    place = (8 * lax.axis_index("gx") + lax.axis_index("gy")).astype(jnp.int32).reshape(1)
    place, concentration = lax.optimization_barrier((place, concentration))
    frame = shaped(ROWS, NZ, LANES)
    smem, anywhere = pl.BlockSpec(memory_space=pltpu.SMEM), pl.BlockSpec(memory_space=pl.ANY)
    scratch = lambda *shape: pltpu.VMEM(shape, jnp.float32)
    line_scratch = scratch(MZ * CX, CY)
    table_scratch = [scratch(5 * CX, LANES)] * 2

    kept = lambda array: pltpu.with_memory_space_constraint(array, pltpu.HBM)
    hbm = pl.BlockSpec(memory_space=pltpu.HBM)
    own, *far = pl.pallas_call(
        own_kernel,
        out_shape=[shaped(2, CX, NZ, CY)] + [shaped(2, FAR, NZ, CY)] * 2,
        in_specs=[smem, hbm, hbm],
        out_specs=vmem(3),
        scratch_shapes=[scratch(NZ, CX, CY), pltpu.VMEM((NZ, CX, CY), jnp.int32), pltpu.SemaphoreType.DMA((2,))],
        compiler_params=room(4),
        name="own",
    )(place, kept(concentration), kept(labels))
    parts = (*swapped(own, "gx", 1), *swapped(far, "gx", 2), own)
    strips = pl.pallas_call(
        strip_kernel,
        out_shape=[shaped(PACKS, NZ, CY)] * 2,
        in_specs=[smem] + vmem(5),
        out_specs=vmem(2),
        compiler_params=room(4),
        name="strips",
    )(place, *parts)
    strips = swapped(strips, "gy", 1)
    half_frame = shaped(ROWS, NZ, CY)
    table = tables()
    tiled = pl.pallas_call(
        tile_kernel,
        out_shape=[half_frame] * 9 + [shaped(16, CY), shaped(NB, NB * size), shaped(*table.shape)],
        in_specs=[smem] + [hbm] * 4 + vmem(5),
        out_specs=vmem(12),
        scratch_shapes=[pltpu.SMEM((8,), jnp.float32)] * 2 + [pltpu.SemaphoreType.DMA((4,))],
        compiler_params=room(4),
        cost_estimate=cost(10_000_000),
        name="tile",
    )(place, *(kept(a) for a in (curve_scale, curve_slope, coarse_inv[0], jnp.asarray(table))), *parts)
    west0, below0 = tiled[3:5]
    inverse_rows, table = tiled[10:]
    west1, below1, south, inverse, source, partial = pl.pallas_call(
        setup_kernel,
        out_shape=[half_frame] * 2 + [frame] * 3 + [shaped(n_y, WINDOW, CY)],
        in_specs=[smem] + vmem(14),
        out_specs=vmem(6),
        scratch_shapes=[scratch(ROWS, NZ, CY)] * 3 + [line_scratch],
        compiler_params=room(8),
        name="setup",
    )(place, *tiled, *strips)
    faces = (west0, west1, south, below0, below1)

    residual, update = source, None
    for sweep, reach in enumerate(REACH):
        through = lax.all_to_all(partial, "gx", 0, 0, tiled=True, axis_index_groups=along_y)
        turned = pl.pallas_call(
            turn_kernel,
            out_shape=shaped(N_Z, SPAN, CY),
            in_specs=vmem(1),
            out_specs=vmem(1)[0],
            compiler_params=room(4),
            name="turn",
        )(through)
        arrived = lax.all_to_all(turned, "gx", 0, 0, tiled=True, axis_index_groups=along_z)
        answer = pl.pallas_call(
            answer_kernel,
            out_shape=shaped(SPAN, CY),
            in_specs=vmem(1),
            out_specs=vmem(1)[0],
            compiler_params=room(4),
            name="answer",
        )(arrived)
        one, two = swapped(answer, "gy", 1)
        local = pl.pallas_call(
            functools.partial(local_kernel, wide=reach + 1),
            out_shape=frame,
            in_specs=[anywhere] + vmem(7),
            out_specs=vmem(1)[0],
            scratch_shapes=[scratch(3, CX + 2 * OV, NZ, LANES)] * 3,
            compiler_params=room(8),
            cost_estimate=cost(20_000_000),
            name="local",
        )(answer, residual, *faces, inverse)
        operands = [place, one, answer, two, local, source, *faces, table]
        operands += [] if sweep == 0 else [update]
        kernel = functools.partial(update_kernel, reach=reach, first=sweep == 0)
        if reach:
            operands += [inverse_rows]
            update, residual, partial = pl.pallas_call(
                kernel,
                out_shape=[frame, frame, shaped(n_y, WINDOW, CY)],
                in_specs=[smem] + vmem(len(operands) - 1),
                out_specs=vmem(3),
                scratch_shapes=table_scratch + [line_scratch],
                compiler_params=room(8),
                name="update",
            )(*operands)
        else:
            operands += [own]
            return pl.pallas_call(
                kernel,
                out_shape=[shaped(NZ, CX, CY)] * 2,
                in_specs=[smem] + vmem(len(operands) - 1),
                out_specs=vmem(2),
                scratch_shapes=table_scratch,
                compiler_params=room(8),
                name="final",
            )(*operands)


def solution(mesh):
    return jax.shard_map(
        on_device,
        mesh=mesh,
        in_specs=(P(None, "gx", "gy"), P(None, "gx", "gy"), P(), P(), P("gy", "gx", None)),
        out_specs=(P(None, "gx", "gy"), P(None, "gx", "gy")),
        check_vma=False,
    )
```
